32 devices in a mesh: doc: 4 (over z), feat: 8 (over y, x, core).
Axes of the slice: x: 2, y: 2, z: 4, core: 2. Of those that a mesh axis runs over, the one named last changes fastest.
Arguments:
- documents: bfloat16 [512, 512], P('doc', 'feat'), may hold values from -6 to 6
- directions: bfloat16 [512, 32768], P('doc', 'feat'), may hold values from -0.5 to 0.5
- phase: float32 [32768], P('feat'), may hold values from -3.140625 to 3.140625
- amplitude: float32 [32768], P('feat'), may hold values from 0.4 to 2.3
- doc_weight: float32 [512], P('doc'), may hold values from 0.5 to 4.2
- labels: int32 [512], P('doc'), may hold values from 0 to 127
Outputs:
- margins: float32 [512, 128], P('doc')
- scaled_weights: float32 [32768, 128], P('feat')
The draws below stay inside these ranges and needn't reach their ends.
All inputs are finite; a program needn't handle non-finite values.
Results may differ from the reference program's by a relative error of at most 0.0003.
Values may be sent and summed in bfloat16 or wider, within the bound.
A program may use at most 64 MiB of HBM per device.

```python
import jax
import jax.numpy as jnp
from jax import lax

F = 512
W = 32768
C = 128
DOC_DEV = 128
ITERS = 3
NEWTON = 3
NDOC = 512
N_DOC = 4
N_FEAT = 8


def draw_amplitude(key, part):
    ramp = 0.6 + 1.2 * jnp.arange(W, dtype=jnp.float32) / (W - 1)
    spread = jax.random.uniform(key, (W,), jnp.float32, 0.8, 1.2)
    return ramp * spread


def draw_doc_weight(key, part):
    ramp = 1.0 + 2.0 * jnp.arange(NDOC, dtype=jnp.float32) / (NDOC - 1)
    spread = jax.random.uniform(key, (NDOC,), jnp.float32, 0.7, 1.3)
    return ramp * spread


def with_ends(entries, own_key, smallest, high):
    longest = entries.shape.index(max(entries.shape))
    spots = []
    for shift in (0, 1):
        where = [jax.random.randint(jax.random.fold_in(own_key, axis), (), 0, length) for axis, length in enumerate(entries.shape)]
        where[longest] = (where[longest] + shift) % entries.shape[longest]
        spots.append(tuple(where))
    return entries.at[spots[0]].set(smallest).at[spots[1]].set(high)


def block_scale(key, extent, shards, smallest, largest):
    def one(position, parts):
        heights = jax.random.uniform(jax.random.fold_in(jax.random.fold_in(key, 6), position), (parts,), jnp.float32, smallest / len(shards), largest / len(shards))
        return jnp.repeat(jnp.exp(heights), extent[position] // parts).reshape((-1,) + (1,) * (len(extent) - position - 1))

    level = one(*shards[0])
    for cut in shards[1:]:
        level = level * one(*cut)
    return level


def normal_values(stream_key, shape, width, most, shards=(), held_as=jnp.bfloat16):
    values = width * jax.random.normal(stream_key, shape, jnp.float32)
    if shards:
        values = values * block_scale(stream_key, shape, shards, -0.22, 0.18)
    return jnp.clip(values, -most, most).astype(held_as)


def setup_inputs(seed: int = 0) -> dict:
    keys = jax.random.split(jax.random.key(seed), 7)
    documents = normal_values(keys[0], (NDOC, F), 1.0, 6.0, ((0, 4), (1, 8)))
    directions = normal_values(keys[1], (F, W), (F // 4) ** -0.5, 0.5, ((0, 4), (1, 8)))
    phase = jnp.clip(jax.random.uniform(keys[2], (W,), jnp.float32, -3.140625, 3.140625), -3.140625, 3.140625)
    amplitude = draw_amplitude(jax.random.fold_in(keys[6], 71), 0)
    doc_weight = draw_doc_weight(jax.random.fold_in(keys[6], 71), 0)
    labels = with_ends(jax.random.randint(keys[5], (NDOC,), 0, C), jax.random.fold_in(keys[5], 1), 0, C - 1).astype(jnp.int32)
    return dict(documents=documents, directions=directions, phase=phase, amplitude=amplitude, doc_weight=doc_weight, labels=labels)


shrink_level = 0.1
ratio_floor = 1e-06

def feature_tile(documents, directions, phase, amplitude, row_block, col_block):
    width_tile = W // N_FEAT
    doc_rows = lax.dynamic_slice_in_dim(documents, (row_block * DOC_DEV).astype(jnp.int32), DOC_DEV, 0)
    dir_cols = lax.dynamic_slice_in_dim(directions, (col_block * width_tile).astype(jnp.int32), width_tile, 1)
    phase_cols = lax.dynamic_slice_in_dim(phase, (col_block * width_tile).astype(jnp.int32), width_tile, 0)
    amp_cols = lax.dynamic_slice_in_dim(amplitude, (col_block * width_tile).astype(jnp.int32), width_tile, 0)
    angles = jnp.dot(doc_rows.astype(jnp.float32), dir_cols.astype(jnp.float32), preferred_element_type=jnp.float32)
    return jnp.sqrt(2.0 / width_tile) * amp_cols * jnp.cos(angles + phase_cols)

def project_tile(features, factor, start, target):
    residue = target - jnp.dot(features, start, precision=lax.Precision.HIGHEST)
    halfway = lax.linalg.triangular_solve(factor, residue, left_side=True, lower=True)
    solved = lax.linalg.triangular_solve(factor, halfway, left_side=True, lower=True, transpose_a=True)
    new_copy = start + lax.dot_general(features, solved, (((0,), (0,)), ((), ())), precision=lax.Precision.HIGHEST)
    new_part = jnp.dot(features, new_copy, precision=lax.Precision.HIGHEST)
    return (new_copy, new_part)

def logistic_prox(target, signs, weight_ratio):
    current = target
    for newton_step in range(NEWTON):
        chance = jax.nn.sigmoid(-signs * current)
        gradient = current - target - weight_ratio * signs * chance
        current = current - gradient / (1.0 + weight_ratio * chance * (1.0 - chance))
    return current

def shrink_values(target, limit):
    return target - jnp.clip(target, -limit, limit)

def reference(documents, directions, phase, amplitude, doc_weight, labels):
    width_tile = W // N_FEAT
    tile_count = N_DOC * N_FEAT
    tile_index = jnp.arange(tile_count, dtype=jnp.int32)

    def factor_tile(tile):
        features = feature_tile(documents, directions, phase, amplitude, tile // N_FEAT, tile % N_FEAT)
        gram = jnp.eye(DOC_DEV, dtype=jnp.float32) + lax.dot_general(features, features, (((1,), (1,)), ((), ())), precision=lax.Precision.HIGHEST)
        return jnp.linalg.cholesky(gram)
    factors = lax.map(factor_tile, tile_index)
    signs = jnp.where(labels[:, None] == jnp.arange(C, dtype=jnp.int32)[None, :], 1.0, -1.0).astype(jnp.float32)
    loss_weight = doc_weight[:, None]
    rho = jnp.float32(1.0)
    margins = logistic_prox(jnp.zeros((NDOC, C), jnp.float32), signs, loss_weight / rho)
    sums = jnp.zeros((NDOC, C), jnp.float32)
    duals_y = jnp.zeros((NDOC, C), jnp.float32)
    duals_x = jnp.zeros((N_DOC, N_FEAT, width_tile, C), jnp.float32)
    partial_value = jnp.zeros((N_DOC, N_FEAT, DOC_DEV, C), jnp.float32)
    weights = jnp.zeros((N_FEAT, width_tile, C), jnp.float32)
    for step in range(ITERS):
        fix_blocks = ((margins - duals_y - sums) / N_FEAT).reshape(N_DOC, DOC_DEV, C)

        def tile_step(tile):
            row_block = tile // N_FEAT
            col_block = tile % N_FEAT
            features = feature_tile(documents, directions, phase, amplitude, row_block, col_block)
            start = weights[col_block] - duals_x[row_block, col_block]
            target = partial_value[row_block, col_block] + fix_blocks[row_block]
            return project_tile(features, factors[tile], start, target)
        new_copy, new_part = lax.map(tile_step, tile_index)
        new_copy = new_copy.reshape(N_DOC, N_FEAT, width_tile, C)
        partial_value = new_part.reshape(N_DOC, N_FEAT, DOC_DEV, C)
        sums = lax.optimization_barrier(jnp.sum(partial_value, axis=1)).reshape(NDOC, C)
        old_weights = weights
        old_margins = margins
        weights = shrink_values(lax.optimization_barrier(jnp.sum(new_copy + duals_x, axis=0)) / N_DOC, shrink_level / (rho * N_DOC))
        margins = logistic_prox(sums + duals_y, signs, loss_weight / rho)
        duals_x = duals_x + new_copy - weights[None]
        duals_y = duals_y + sums - margins
        if step + 1 < ITERS:
            primal = jnp.sum((new_copy - weights[None]) ** 2) + jnp.sum((sums - margins) ** 2)
            dual_norm = rho * rho * (N_DOC * jnp.sum((weights - old_weights) ** 2) + jnp.sum((margins - old_margins) ** 2))
            growth = ((primal + ratio_floor) / (dual_norm + ratio_floor)) ** 0.25
            rho = rho * growth
            duals_x = duals_x / growth
            duals_y = duals_y / growth
    return (margins, N_FEAT * weights.reshape(W, C))
```

```python
import functools

import jax
import jax.numpy as jnp
from jax import lax
from jax.experimental import pallas as pl
from jax.experimental.pallas import tpu as pltpu
from jax.sharding import PartitionSpec as P

C = 128
ITERS = 3
NEWTON = 3
LEVELS = 32767.0
HI = lax.Precision.HIGHEST
MESH = pl.DeviceIdType.MESH

shrink_level = 0.1
ratio_floor = 1e-06


def logistic_prox(target, signs, weight_ratio):
    current = target
    for newton_step in range(NEWTON):
        chance = 1.0 / (1.0 + jnp.exp(signs * current))
        gradient = current - target - weight_ratio * signs * chance
        current = current - gradient / (1.0 + weight_ratio * chance * (1.0 - chance))
    return current


def shrink_values(target, limit):
    return target - jnp.minimum(jnp.maximum(target, -limit), limit)


def cosine(angle):
    turns = jnp.floor(angle * 0.3183098861837907 + 0.5)
    rest = angle - turns * 3.140625
    rest = rest - turns * 9.67502593994140625e-4
    rest = rest - turns * 1.509957990978376432e-7
    odd = turns - 2.0 * jnp.floor(turns * 0.5)
    sq = rest * rest
    poly = 2.08767569878681e-9
    poly = poly * sq - 2.755731922398589e-7
    poly = poly * sq + 2.48015873015873e-5
    poly = poly * sq - 1.388888888888889e-3
    poly = poly * sq + 4.1666666666666664e-2
    poly = poly * sq - 0.5
    poly = poly * sq + 1.0
    return poly * (1.0 - 2.0 * odd)


def split(values):
    high = values.astype(jnp.bfloat16)
    return high, (values - high.astype(jnp.float32)).astype(jnp.bfloat16)


def split_dot(high, low, pair):
    both = jnp.dot(high, pair, preferred_element_type=jnp.float32)
    rest = jnp.dot(low, pair[:, :C], preferred_element_type=jnp.float32)
    return both[:, :C] + (both[:, C:] + rest)


def encode(values):
    largest = jnp.max(jnp.abs(values), axis=0, keepdims=True)
    steps = jnp.where(largest > 0.0, LEVELS / largest, 0.0)
    codes = jnp.floor(values * steps + 0.5).astype(jnp.int32).astype(jnp.int16)
    return codes, largest * (1.0 / LEVELS)


def decode(codes, steps):
    return codes.astype(jnp.int32).astype(jnp.float32) * steps


def remote(src, dst, send_sem, recv_sem, axis, peer):
    return pltpu.make_async_remote_copy(
        src_ref=src,
        dst_ref=dst,
        send_sem=send_sem,
        recv_sem=recv_sem,
        device_id={axis: peer},
        device_id_type=MESH,
    )


def greet(num_doc, num_feat):
    barrier = pltpu.get_barrier_semaphore()
    for axis, size in (("doc", num_doc), ("feat", num_feat)):
        me = lax.axis_index(axis)
        for k in range(1, size):
            pl.semaphore_signal(
                barrier, inc=1, device_id={axis: lax.rem(me + k, size)}, device_id_type=MESH
            )
    pl.semaphore_wait(barrier, num_doc + num_feat - 2)


class Channel:
    def __init__(self, sems, axis, size):
        self.sems, self.axis, self.size = sems, axis, size
        self.me = lax.axis_index(axis)
        self.pending = []

    def peers(self):
        return [lax.rem(self.me + k, self.size) for k in range(1, self.size)]

    def send(self, slot, peer, src, dst):
        copy = remote(
            src, dst, self.sems.at[0, slot, peer], self.sems.at[1, slot, self.me], self.axis, peer
        )
        copy.start()
        self.pending.append(copy)

    def arrived(self, slot, peer, ref):
        remote(
            ref, ref, self.sems.at[0, slot, peer], self.sems.at[1, slot, peer], self.axis, peer
        ).wait_recv()

    def drain(self):
        for copy in self.pending:
            copy.wait_send()


def build_kernel(
    num_doc, num_feat, subs, scale,
    docs_ref, dir_ref, phase_hbm, amp_hbm,
    feat_ref, featt_ref, gram_ref,
    dpart, phase_ref, amp_ref, dirs, gsend, grecv,
    part_sems, row_sems, dir_sems, gram_sems, local_sem, table_sems,
):
    n = docs_ref.shape[1]
    chunk = dirs.shape[2]
    wide = chunk // subs
    me = lax.axis_index("doc")
    fme = lax.axis_index("feat")
    tables = [
        pltpu.make_async_copy(docs_ref, dpart.at[fme, me], table_sems.at[2]),
        pltpu.make_async_copy(phase_hbm.at[me], phase_ref, table_sems.at[0]),
        pltpu.make_async_copy(amp_hbm.at[me], amp_ref, table_sems.at[1]),
    ]
    for table in tables:
        table.start()
    local = pltpu.make_async_copy(
        dir_ref.at[:, pl.ds(pl.multiple_of(me * chunk, chunk), chunk)], dirs.at[me], local_sem
    )
    local.start()
    greet(num_doc, num_feat)
    ch_part = Channel(part_sems, "feat", num_feat)
    ch_row = Channel(row_sems, "doc", num_doc)
    ch_dir = Channel(dir_sems, "doc", num_doc)
    ch_gram = Channel(gram_sems, "doc", num_doc)
    for peer in ch_row.peers():
        ch_row.send(0, peer, docs_ref, dpart.at[fme, me])
    for s in range(subs):
        for peer in ch_dir.peers():
            cols = pl.ds(pl.multiple_of(peer * chunk + s * wide, wide), wide)
            ch_dir.send(
                s, peer, dir_ref.at[:, cols], dirs.at[me, :, pl.ds(s * wide, wide)]
            )
    tables[0].wait()
    for peer in ch_row.peers():
        ch_row.arrived(0, peer, dpart.at[fme, peer])
    for peer in ch_part.peers():
        ch_part.send(0, peer, dpart.at[fme], dpart.at[fme])
    for peer in ch_part.peers():
        ch_part.arrived(0, peer, dpart.at[peer])
    inputs = num_feat * docs_ref.shape[0]
    full = jnp.concatenate([dpart[:, i].reshape(inputs, n).T for i in range(num_doc)], axis=0)
    local.wait()
    for table in tables[1:]:
        table.wait()
    phase = phase_ref[...]
    amp = scale * amp_ref[...]
    for s in range(subs):
        cols = slice(s * wide, (s + 1) * wide)
        for peer in ch_dir.peers():
            ch_dir.arrived(s, peer, dirs.at[peer, :, pl.ds(s * wide, wide)])
        piece = dirs[:, :, cols].reshape(full.shape[1], wide)
        angles = jnp.dot(full, piece, preferred_element_type=jnp.float32)
        feats = amp[:, cols] * cosine(angles + phase[:, cols])
        flipped = feats.T
        feat_ref[0, :, cols], feat_ref[1, :, cols] = split(feats)
        featt_ref[0, cols, :], featt_ref[1, cols, :] = split(flipped)
        for i in range(num_doc):
            block = feats[i * n : (i + 1) * n]
            term = lax.dot_general(block, block, (((1,), (1,)), ((), ())), precision=HI)
            if s == 0:
                gsend[i] = term
            else:
                gsend[i] += term
    for peer in ch_gram.peers():
        ch_gram.send(0, peer, gsend.at[peer], grecv.at[me])
    grecv[me] = gsend[me]
    for peer in ch_gram.peers():
        ch_gram.arrived(0, peer, grecv.at[peer])
    total = grecv[0]
    for i in range(1, num_doc):
        total += grecv[i]
    rows = lax.broadcasted_iota(jnp.int32, (n, n), 0)
    cols = lax.broadcasted_iota(jnp.int32, (n, n), 1)
    gram_ref[...] = total + jnp.where(rows == cols, 1.0, 0.0)
    for channel in (ch_part, ch_row, ch_dir, ch_gram):
        channel.drain()


def sweep_kernel(gram_ref, inverse_ref):
    values = gram_ref[...]
    n = values.shape[0]
    lanes = lax.broadcasted_iota(jnp.int32, (1, n), 1)
    rows = lax.broadcasted_iota(jnp.int32, (n, 1), 0)
    for k in range(n):
        pivot = 1.0 / values[k : k + 1, k : k + 1]
        row = jnp.where(lanes == k, pivot, values[k : k + 1, :] * pivot)
        column = values[:, k : k + 1]
        values = jnp.where(
            rows == k, row, jnp.where(lanes == k, 0.0, values) - column * row
        )
    inverse_ref[...] = values


def fold(values):
    return jnp.sum(values.reshape(values.shape[0] // 8, 8, values.shape[1]), axis=0)


def total(values):
    return jnp.sum(jnp.sum(values, axis=0, keepdims=True), axis=1, keepdims=True)


def admm_kernel(
    num_doc, num_feat, subs,
    feat_ref, featt_ref, inv_ref, lab_hbm, dw_hbm,
    m_ref, w_ref, wstep_ref, lab_ref, dw_ref, small_sems,
    solved, solved_step, part, yrecv, cbuf, psend, psend_step, precv, precv_step,
    sc1, sc2, z, lastmove, lastlift, signs_ref, weight_ref, wown, wown_step,
    s_sems, y_sems, c_sems, p_sems, sc1_sems, sc2_sems, w_sems, wown_sems,
):
    n = inv_ref.shape[0]
    chunk = z.shape[0]
    share = n // num_feat
    wide = chunk // subs
    me = lax.axis_index("doc")
    fme = lax.axis_index("feat")
    ch_s = Channel(s_sems, "doc", num_doc)
    ch_y = Channel(y_sems, "feat", num_feat)
    ch_c = Channel(c_sems, "feat", num_feat)
    ch_p = Channel(p_sems, "doc", num_doc)
    ch_1 = Channel(sc1_sems, "doc", num_doc)
    ch_2 = Channel(sc2_sems, "feat", num_feat)
    smalls = [
        pltpu.make_async_copy(lab_hbm, lab_ref, small_sems.at[0]),
        pltpu.make_async_copy(dw_hbm, dw_ref, small_sems.at[1]),
    ]
    for small in smalls:
        small.start()
    for small in smalls:
        small.wait()
    classes = lax.broadcasted_iota(jnp.int32, (n, C), 1).astype(jnp.float32)
    spread = jnp.broadcast_to(lab_ref[...].astype(jnp.float32), (C, n)).T
    all_weight = jnp.broadcast_to(dw_ref[...], (C, n)).T
    all_signs = jnp.where(spread == classes, 1.0, -1.0)
    start = logistic_prox(jnp.zeros((n, C), jnp.float32), all_signs, all_weight)
    signs_ref[...] = all_signs
    weight_ref[...] = all_weight
    own = pl.ds(pl.multiple_of(fme * share, share), share)
    signs = signs_ref[own, :]
    weight = weight_ref[own, :]
    margins = logistic_prox(jnp.zeros((share, C), jnp.float32), signs, weight)
    duals = jnp.zeros((share, C), jnp.float32)
    rho = jnp.ones((1, 1), jnp.float32)
    inv = inv_ref[...]
    target = start / num_feat
    residue = target
    growth = None

    def my_rows(src, s):
        return pl.ds(pl.multiple_of(src * chunk + s * wide, wide), wide)

    groups = wown_step.shape[1]
    rows_per = wide // groups

    def w_copy(direction, src, s, peer, own=False):
        codes = w_ref.at[my_rows(src, s), :]
        steps = wstep_ref.at[src, s]
        return [
            remote(
                wown.at[s] if own else codes, codes,
                w_sems.at[direction, 0, 0, src, s], w_sems.at[direction, 0, 1, src, s], "doc", peer,
            ),
            remote(
                wown_step.at[s] if own else steps, steps,
                w_sems.at[direction, 1, 0, src, s], w_sems.at[direction, 1, 1, src, s], "doc", peer,
            ),
        ]

    def keep_own(s):
        return [
            pltpu.make_async_copy(wown.at[s], w_ref.at[my_rows(me, s), :], wown_sems.at[0, s]),
            pltpu.make_async_copy(wown_step.at[s], wstep_ref.at[me, s], wown_sems.at[1, s]),
        ]

    for step in range(ITERS):
        last = step + 1 == ITERS
        answer = jnp.dot(inv, residue, precision=HI)
        applied = residue - answer
        new_part = target - answer
        solved[step, me], solved_step[step, me] = encode(answer)
        part[step] = new_part
        for peer in ch_s.peers():
            ch_s.send(2 * step, peer, solved.at[step, me], solved.at[step, me])
            ch_s.send(2 * step + 1, peer, solved_step.at[step, me], solved_step.at[step, me])
        for peer in ch_y.peers():
            rows = pl.ds(pl.multiple_of(peer * share, share), share)
            ch_y.send(step, peer, part.at[step, rows, :], yrecv.at[step, fme])
        yrecv[step, fme] = part[step, own, :]
        for peer in ch_y.peers():
            ch_y.arrived(step, peer, yrecv.at[step, peer])
        sums = yrecv[step, 0]
        for k in range(1, num_feat):
            sums += yrecv[step, k]
        old_margins = margins
        margins = logistic_prox(sums + duals, signs, weight / rho)
        duals = duals + sums - margins
        cbuf[step, fme, 0] = margins if last else (margins - sums) / num_feat
        cbuf[step, fme, 1] = duals / num_feat
        for peer in ch_c.peers():
            ch_c.send(step, peer, cbuf.at[step, fme], cbuf.at[step, fme])
        for peer in ch_s.peers():
            ch_s.arrived(2 * step, peer, solved.at[step, peer])
            ch_s.arrived(2 * step + 1, peer, solved_step.at[step, peer])
        everything = jnp.concatenate(
            split(decode(solved[step], solved_step[step]).reshape(num_doc * n, C)), axis=1
        )
        limit = shrink_level / (rho * num_doc)
        if not last:
            gap = fold((sums - margins) ** 2) if share > 8 else (sums - margins) ** 2
            shift = (
                fold((margins - old_margins) ** 2) if share > 8 else (margins - old_margins) ** 2
            )
            if step == 0:
                d_answer, d_applied = answer, applied
            else:
                d_answer = answer - last_answer / growth
                d_applied = applied - last_applied / growth
            primal = gap + fold(d_answer * d_applied)
            dual = shift
        for s in range(subs):
            rows = slice(s * wide, (s + 1) * wide)
            lift = split_dot(featt_ref[0, rows, :], featt_ref[1, rows, :], everything)
            if step == 0:
                fresh = shrink_values(lift / num_doc, limit)
                move = -fresh
                d_move, d_lift = move, lift
            else:
                old = z[rows, :]
                fresh = shrink_values(old + lift / num_doc, limit)
                if not last:
                    move = old - fresh
                    d_move = move - lastmove[rows, :] / growth
                    d_lift = lift - lastlift[rows, :] / growth
            if last:
                for g in range(groups):
                    piece = slice(g * rows_per, (g + 1) * rows_per)
                    wown[s, piece, :], wown_step[s, g] = encode(num_feat * fresh[piece])

                @pl.when(me + 1 < num_doc)
                def _(s=s):
                    for copy in w_copy(0, me, s, me + 1, own=True):
                        copy.start()

                @pl.when(me >= 1)
                def _(s=s):
                    for copy in w_copy(1, me, s, me - 1, own=True):
                        copy.start()

                for copy in keep_own(s):
                    copy.start()
            else:
                z[rows, :] = fresh
                lastmove[rows, :] = move
                lastlift[rows, :] = lift
                primal += fold(num_doc * d_move * d_move + 2.0 * d_move * d_lift)
                dual += num_doc * fold(move * move)
        if last:
            break
        sc1[step, me, 0] = primal
        sc1[step, me, 1] = dual
        for peer in ch_1.peers():
            ch_1.send(step, peer, sc1.at[step, me], sc1.at[step, me])
        weights = jnp.concatenate(split(z[...]), axis=1)
        for k in range(1, num_doc + 1):
            peer = lax.rem(me + k, num_doc)
            block = pl.ds(pl.multiple_of(peer * n, n), n)
            product = split_dot(feat_ref[0, block, :], feat_ref[1, block, :], weights)
            if k < num_doc:
                psend[step, k - 1], psend_step[step, k - 1] = encode(product)
                ch_p.send(2 * step, peer, psend.at[step, k - 1], precv.at[step, me])
                ch_p.send(2 * step + 1, peer, psend_step.at[step, k - 1], precv_step.at[step, me])
        for peer in ch_1.peers():
            ch_1.arrived(step, peer, sc1.at[step, peer])
        both = sc1[step, 0]
        for i in range(1, num_doc):
            both += sc1[step, i]
        sc2[step, fme] = both
        for peer in ch_2.peers():
            ch_2.send(step, peer, sc2.at[step, fme], sc2.at[step, fme])
        for peer in ch_2.peers():
            ch_2.arrived(step, peer, sc2.at[step, peer])
        both = sc2[step, 0]
        for k in range(1, num_feat):
            both += sc2[step, k]
        primal = jnp.maximum(total(both[0]), 0.0)
        dual = total(both[1])
        last_answer, last_applied = answer, applied
        for peer in ch_c.peers():
            ch_c.arrived(step, peer, cbuf.at[step, peer])
        growth = jnp.sqrt(
            jnp.sqrt((primal + ratio_floor) / (rho * rho * dual + ratio_floor))
        )
        rho = rho * growth
        duals = duals / growth
        fixed = cbuf[step, :, 0].reshape(n, C) - cbuf[step, :, 1].reshape(n, C) / growth
        target = new_part + fixed
        for peer in ch_p.peers():
            ch_p.arrived(2 * step, peer, precv.at[step, peer])
            ch_p.arrived(2 * step + 1, peer, precv_step.at[step, peer])
            product += decode(precv[step, peer], precv_step[step, peer])
        previous = jnp.zeros((n, C), jnp.float32) if step == 0 else old_product
        residue = target - (product - (previous - product + applied) / growth)
        old_product = product
    for hop in range(1, num_doc):
        for s in range(subs):

            @pl.when(me >= hop)
            def _(hop=hop, s=s):
                for copy in w_copy(0, me - hop, s, me):
                    copy.wait_recv()

                @pl.when(me + 1 < num_doc)
                def _():
                    for copy in w_copy(0, me - hop, s, me + 1):
                        copy.start()

            @pl.when(me + hop < num_doc)
            def _(hop=hop, s=s):
                for copy in w_copy(1, me + hop, s, me):
                    copy.wait_recv()

                @pl.when(me >= 1)
                def _():
                    for copy in w_copy(1, me + hop, s, me - 1):
                        copy.start()

    for peer in ch_c.peers():
        ch_c.arrived(ITERS - 1, peer, cbuf.at[ITERS - 1, peer])
    m_ref[...] = cbuf[ITERS - 1, :, 0].reshape(n, C)
    for s in range(subs):
        for copy in keep_own(s):
            copy.wait()
    for hop in range(num_doc):
        for s in range(subs):

            @pl.when((me >= hop) & (me + 1 < num_doc))
            def _(hop=hop, s=s):
                for copy in w_copy(0, me - hop, s, me + 1):
                    copy.wait_send()

            @pl.when((me + hop < num_doc) & (me >= 1))
            def _(hop=hop, s=s):
                for copy in w_copy(1, me + hop, s, me - 1):
                    copy.wait_send()

    for channel in (ch_s, ch_y, ch_c, ch_p, ch_1, ch_2):
        channel.drain()


def whole_kernel(
    num_doc, num_feat, subs, scale,
    docs_ref, dir_ref, phase_hbm, amp_hbm, lab_ref, dw_ref,
    m_ref, w_ref, wstep_ref,
    feat_ref, featt_ref, gram_ref, inv_ref,
    *scratch,
):
    build_kernel(
        num_doc, num_feat, subs, scale,
        docs_ref, dir_ref, phase_hbm, amp_hbm, feat_ref, featt_ref, gram_ref, *scratch[:12],
    )
    sweep_kernel(gram_ref, inv_ref)
    admm_kernel(
        num_doc, num_feat, subs,
        feat_ref, featt_ref, inv_ref, lab_ref, dw_ref, m_ref, w_ref, wstep_ref, *scratch[12:],
    )


def per_device(documents, directions, phase, amplitude, doc_weight, labels):
    n, local_inputs = documents.shape
    input_rows, width_tile = directions.shape
    num_feat = lax.axis_size("feat")
    num_doc = lax.axis_size("doc")
    chunk = width_tile // num_doc
    subs = max(1, min(4, chunk // 128))
    share = n // num_feat
    f32, bf16 = jnp.float32, jnp.bfloat16
    vmem = pl.BlockSpec(memory_space=pltpu.VMEM)
    dma = pltpu.SemaphoreType.DMA
    shape = jax.ShapeDtypeStruct
    rounds = ITERS - 1
    hbm = pl.BlockSpec(memory_space=pltpu.HBM)
    groups = max(1, chunk // subs // n)
    margins, codes, steps = pl.pallas_call(
        functools.partial(
            whole_kernel, num_doc, num_feat, subs, (2.0 / width_tile) ** 0.5
        ),
        out_shape=(
            shape((n, C), f32),
            shape((width_tile, C), jnp.int16),
            shape((num_doc, subs, groups, 1, C), f32),
        ),
        in_specs=[hbm] * 6,
        out_specs=(vmem, hbm, hbm),
        scratch_shapes=[
            pltpu.VMEM((2, num_doc * n, chunk), bf16),
            pltpu.VMEM((2, chunk, num_doc * n), bf16),
            pltpu.VMEM((n, n), f32),
            pltpu.VMEM((n, n), f32),
            pltpu.VMEM((num_feat, num_doc, local_inputs, n), bf16),
            pltpu.VMEM((1, chunk), f32),
            pltpu.VMEM((1, chunk), f32),
            pltpu.VMEM((num_doc, input_rows, chunk), bf16),
            pltpu.VMEM((num_doc, n, n), f32),
            pltpu.VMEM((num_doc, n, n), f32),
            dma((2, 1, num_feat)),
            dma((2, 1, num_doc)),
            dma((2, subs, num_doc)),
            dma((2, 1, num_doc)),
            dma,
            dma((3,)),
            pltpu.VMEM((1, n), jnp.int32),
            pltpu.VMEM((1, n), f32),
            dma((2,)),
            pltpu.VMEM((ITERS, num_doc, n, C), jnp.int16),
            pltpu.VMEM((ITERS, num_doc, 1, C), f32),
            pltpu.VMEM((ITERS, n, C), f32),
            pltpu.VMEM((ITERS, num_feat, share, C), f32),
            pltpu.VMEM((ITERS, num_feat, 2, share, C), f32),
            pltpu.VMEM((rounds, num_doc, n, C), jnp.int16),
            pltpu.VMEM((rounds, num_doc, 1, C), f32),
            pltpu.VMEM((rounds, num_doc, n, C), jnp.int16),
            pltpu.VMEM((rounds, num_doc, 1, C), f32),
            pltpu.VMEM((rounds, num_doc, 2, 8, C), f32),
            pltpu.VMEM((rounds, num_feat, 2, 8, C), f32),
            pltpu.VMEM((chunk, C), f32),
            pltpu.VMEM((chunk, C), f32),
            pltpu.VMEM((chunk, C), f32),
            pltpu.VMEM((n, C), f32),
            pltpu.VMEM((n, C), f32),
            pltpu.VMEM((subs, chunk // subs, C), jnp.int16),
            pltpu.VMEM((subs, groups, 1, C), f32),
            dma((2, 2 * ITERS, num_doc)),
            dma((2, ITERS, num_feat)),
            dma((2, ITERS, num_feat)),
            dma((2, 2 * rounds, num_doc)),
            dma((2, rounds, num_doc)),
            dma((2, rounds, num_feat)),
            dma((2, 2, 2, num_doc, subs)),
            dma((2, subs)),
        ],
        compiler_params=pltpu.CompilerParams(
            collective_id=0, has_side_effects=True, vmem_limit_bytes=56 * 1024 * 1024
        ),
        name="admm",
    )(
        documents.T,
        directions,
        phase.reshape(num_doc, 1, chunk),
        amplitude.reshape(num_doc, 1, chunk),
        labels.reshape(1, n),
        doc_weight.reshape(1, n),
    )
    tiles = num_doc * subs * groups
    weights = codes.reshape(tiles, width_tile // tiles, C).astype(f32) * steps.reshape(tiles, 1, C)
    return margins, weights.reshape(width_tile, C)


def solution(mesh):
    in_specs = (P("doc", "feat"), P("doc", "feat"), P("feat"), P("feat"), P("doc"), P("doc"))
    out_specs = (P("doc", None), P("feat", None))
    return jax.shard_map(
        per_device, mesh=mesh, in_specs=in_specs, out_specs=out_specs, check_vma=False
    )
```

```python
import functools

import jax
import jax.numpy as jnp
from jax import lax
from jax.experimental import pallas as pl
from jax.experimental.pallas import tpu as pltpu
from jax.sharding import PartitionSpec as P

C = 128
ITERS = 3
NEWTON = 3
LEVELS = 32767.0
INVERSE_STEPS = 7
HI = lax.Precision.HIGHEST
MESH = pl.DeviceIdType.MESH

shrink_level = 0.1
ratio_floor = 1e-06


def logistic_prox(target, signs, weight_ratio):
    current = target
    for newton_step in range(NEWTON):
        chance = 1.0 / (1.0 + jnp.exp(signs * current))
        gradient = current - target - weight_ratio * signs * chance
        current = current - gradient / (1.0 + weight_ratio * chance * (1.0 - chance))
    return current


def shrink_values(target, limit):
    return target - jnp.minimum(jnp.maximum(target, -limit), limit)


def cosine(angle):
    turns = jnp.floor(angle * 0.3183098861837907 + 0.5)
    rest = angle - turns * 3.140625
    rest = rest - turns * 9.67502593994140625e-4
    rest = rest - turns * 1.509957990978376432e-7
    odd = turns - 2.0 * jnp.floor(turns * 0.5)
    sq = rest * rest
    poly = 2.08767569878681e-9
    poly = poly * sq - 2.755731922398589e-7
    poly = poly * sq + 2.48015873015873e-5
    poly = poly * sq - 1.388888888888889e-3
    poly = poly * sq + 4.1666666666666664e-2
    poly = poly * sq - 0.5
    poly = poly * sq + 1.0
    return poly * (1.0 - 2.0 * odd)


def split(values):
    high = values.astype(jnp.bfloat16)
    return high, (values - high.astype(jnp.float32)).astype(jnp.bfloat16)


def split_dot(high, low, pair):
    both = jnp.dot(high, pair, preferred_element_type=jnp.float32)
    rest = jnp.dot(low, pair[:, :C], preferred_element_type=jnp.float32)
    return both[:, :C] + (both[:, C:] + rest)


def encode(values):
    largest = jnp.max(jnp.abs(values), axis=0, keepdims=True)
    steps = jnp.where(largest > 0.0, LEVELS / largest, 0.0)
    codes = jnp.floor(values * steps + 0.5).astype(jnp.int32).astype(jnp.int16)
    return codes, largest * (1.0 / LEVELS)


def decode(codes, steps):
    return codes.astype(jnp.int32).astype(jnp.float32) * steps


def remote(src, dst, send_sem, recv_sem, axis, peer):
    return pltpu.make_async_remote_copy(
        src_ref=src,
        dst_ref=dst,
        send_sem=send_sem,
        recv_sem=recv_sem,
        device_id={axis: peer},
        device_id_type=MESH,
    )


def greet(num_doc, num_feat):
    barrier = pltpu.get_barrier_semaphore()
    for axis, size in (("doc", num_doc), ("feat", num_feat)):
        me = lax.axis_index(axis)
        for k in range(1, size):
            pl.semaphore_signal(
                barrier, inc=1, device_id={axis: lax.rem(me + k, size)}, device_id_type=MESH
            )
    pl.semaphore_wait(barrier, num_doc + num_feat - 2)


class Channel:
    def __init__(self, sems, axis, size):
        self.sems, self.axis, self.size = sems, axis, size
        self.me = lax.axis_index(axis)
        self.pending = []

    def peers(self):
        return [lax.rem(self.me + k, self.size) for k in range(1, self.size)]

    def send(self, slot, peer, src, dst):
        copy = remote(
            src, dst, self.sems.at[0, slot, peer], self.sems.at[1, slot, self.me], self.axis, peer
        )
        copy.start()
        self.pending.append(copy)

    def arrived(self, slot, peer, ref):
        remote(
            ref, ref, self.sems.at[0, slot, peer], self.sems.at[1, slot, peer], self.axis, peer
        ).wait_recv()

    def drain(self):
        for copy in self.pending:
            copy.wait_send()


def build_kernel(
    num_doc, num_feat, subs, scale,
    docs_ref, dir_ref, phase_hbm, amp_hbm,
    feat_ref, featt_ref, gram_ref,
    dpart, phase_ref, amp_ref, dirs, gsum, gsend, grecv,
    part_sems, row_sems, dir_sems, gram_sems, local_sem, table_sems,
):
    n = docs_ref.shape[1]
    chunk = dirs.shape[2]
    wide = chunk // subs
    me = lax.axis_index("doc")
    fme = lax.axis_index("feat")
    tables = [
        pltpu.make_async_copy(docs_ref, dpart.at[fme, me], table_sems.at[2]),
        pltpu.make_async_copy(phase_hbm.at[me], phase_ref, table_sems.at[0]),
        pltpu.make_async_copy(amp_hbm.at[me], amp_ref, table_sems.at[1]),
    ]
    for table in tables:
        table.start()
    local = pltpu.make_async_copy(
        dir_ref.at[:, pl.ds(pl.multiple_of(me * chunk, chunk), chunk)], dirs.at[me], local_sem
    )
    local.start()
    greet(num_doc, num_feat)
    ch_part = Channel(part_sems, "feat", num_feat)
    ch_row = Channel(row_sems, "doc", num_doc)
    ch_dir = Channel(dir_sems, "doc", num_doc)
    ch_gram = Channel(gram_sems, "doc", num_doc)
    for peer in ch_row.peers():
        ch_row.send(0, peer, docs_ref, dpart.at[fme, me])
    for s in range(subs):
        for peer in ch_dir.peers():
            cols = pl.ds(pl.multiple_of(peer * chunk + s * wide, wide), wide)
            ch_dir.send(
                s, peer, dir_ref.at[:, cols], dirs.at[me, :, pl.ds(s * wide, wide)]
            )
    tables[0].wait()
    for peer in ch_row.peers():
        ch_row.arrived(0, peer, dpart.at[fme, peer])
    for peer in ch_part.peers():
        ch_part.send(0, peer, dpart.at[fme], dpart.at[fme])
    for peer in ch_part.peers():
        ch_part.arrived(0, peer, dpart.at[peer])
    inputs = num_feat * docs_ref.shape[0]
    full = jnp.concatenate([dpart[:, i].reshape(inputs, n).T for i in range(num_doc)], axis=0)
    local.wait()
    for table in tables[1:]:
        table.wait()
    phase = phase_ref[...]
    amp = scale * amp_ref[...]
    for s in range(subs):
        cols = slice(s * wide, (s + 1) * wide)
        for peer in ch_dir.peers():
            ch_dir.arrived(s, peer, dirs.at[peer, :, pl.ds(s * wide, wide)])
        piece = dirs[:, :, cols].reshape(full.shape[1], wide)
        angles = jnp.dot(full, piece, preferred_element_type=jnp.float32)
        feats = amp[:, cols] * cosine(angles + phase[:, cols])
        high, low = split(feats)
        feat_ref[0, :, cols], feat_ref[1, :, cols] = high, low
        for i in range(num_doc):
            block = slice(i * n, (i + 1) * n)
            term = lax.dot_general(
                high[block],
                jnp.concatenate([high[block], low[block]], axis=0),
                (((1,), (1,)), ((), ())),
                preferred_element_type=jnp.float32,
            )
            if s == 0:
                gsum[i] = term
            else:
                gsum[i] += term
        featt_ref[0, cols, :], featt_ref[1, cols, :] = split(feats.T)
    for k in range(1, num_doc + 1):
        peer = lax.rem(me + k, num_doc)
        mixed = gsum[peer, :, n:]
        gsend[peer] = pack_symmetric(gsum[peer, :, :n] + (mixed + mixed.T))
        if k < num_doc:
            ch_gram.send(0, peer, gsend.at[peer], grecv.at[me])
    total = gsend[me]
    for peer in ch_gram.peers():
        ch_gram.arrived(0, peer, grecv.at[peer])
        total += grecv[peer]
    gram_ref[...] = unpack_symmetric(total)
    for channel in (ch_part, ch_row, ch_dir, ch_gram):
        channel.drain()


def pack_symmetric(values):
    half = values.shape[0] // 2
    rows = lax.broadcasted_iota(jnp.int32, (half, 2 * half), 0)
    lanes = lax.broadcasted_iota(jnp.int32, (half, 2 * half), 1)
    top, bottom = values[:half], values[half:]
    both = jnp.where(lanes <= rows + half, bottom, pltpu.roll(top, half, 1))
    diagonal = jnp.sum(jnp.where(rows == lanes, top, 0.0), axis=0, keepdims=True)
    return jnp.concatenate([both, jnp.broadcast_to(diagonal, (8, 2 * half))], axis=0)


def unpack_symmetric(packed):
    half = packed.shape[0] - 8
    rows = lax.broadcasted_iota(jnp.int32, (half, 2 * half), 0)
    lanes = lax.broadcasted_iota(jnp.int32, (half, 2 * half), 1)
    both, diagonal = packed[:half], packed[half : half + 1]
    flipped = jnp.concatenate([both, both], axis=0).T
    bottom = jnp.where(lanes <= rows + half, both, flipped[half:])
    corner = jnp.where(lanes > rows, pltpu.roll(both, half, 1), flipped[half:])
    corner = jnp.where(lanes == rows, diagonal, corner)
    return jnp.concatenate([jnp.where(lanes >= half, flipped[:half], corner), bottom], axis=0)


def three_left(values):
    high, low = split(values)
    return jnp.concatenate([high, high, low], axis=1)


def three_right(values):
    high, low = split(values)
    return jnp.concatenate([high, low, high], axis=0)


def three_dot(left, right):
    return jnp.dot(left, right, preferred_element_type=jnp.float32)


def invert(gram):
    n = gram.shape[0]
    rows = lax.broadcasted_iota(jnp.int32, (n, n), 0)
    lanes = lax.broadcasted_iota(jnp.int32, (n, n), 1)
    eye = jnp.where(rows == lanes, 1.0, 0.0)
    matrix = gram + eye
    bound = jnp.max(jnp.sum(jnp.abs(matrix), axis=0, keepdims=True), axis=1, keepdims=True)
    first = 2.0 / (1.0 + bound)
    error = (bound - 1.0) / (bound + 1.0)
    near = first * matrix
    guess = first * eye
    for k in range(INVERSE_STEPS):
        scale = 2.0 / (2.0 - error * error)
        error = 0.5 * error * error * scale
        if k == 0:
            moved = jnp.concatenate([first * near, three_dot(three_left(near), three_right(near))], axis=1)
        else:
            moved = three_dot(
                three_left(near), three_right(jnp.concatenate([guess, near], axis=1))
            )
        guess = scale * (2.0 * guess - moved[:, :n])
        near = scale * (2.0 * near - moved[:, n:])
    missing = eye - jnp.dot(matrix, guess, precision=HI)
    return guess + three_dot(three_left(guess), three_right(missing))


def fold(values):
    return jnp.sum(values.reshape(values.shape[0] // 8, 8, values.shape[1]), axis=0)


def total(values):
    return jnp.sum(jnp.sum(values, axis=0, keepdims=True), axis=1, keepdims=True)


def admm_kernel(
    num_doc, num_feat, subs,
    feat_ref, featt_ref, inv_ref, lab_hbm, dw_hbm,
    m_ref, w_ref, lab_ref, dw_ref, small_sems,
    solved, solved_step, part, yrecv, cbuf, psend, psend_step, precv, precv_step,
    sc1, sc2, z, lastmove, lastlift, signs_ref, weight_ref, wcode, wstep,
    s_sems, y_sems, c_sems, p_sems, sc1_sems, sc2_sems, w_sems,
):
    n = inv_ref.shape[0]
    chunk = z.shape[0]
    share = n // num_feat
    wide = chunk // subs
    me = lax.axis_index("doc")
    fme = lax.axis_index("feat")
    ch_s = Channel(s_sems, "doc", num_doc)
    ch_y = Channel(y_sems, "feat", num_feat)
    ch_c = Channel(c_sems, "feat", num_feat)
    ch_p = Channel(p_sems, "doc", num_doc)
    ch_1 = Channel(sc1_sems, "doc", num_doc)
    ch_2 = Channel(sc2_sems, "feat", num_feat)
    smalls = [
        pltpu.make_async_copy(lab_hbm, lab_ref, small_sems.at[0]),
        pltpu.make_async_copy(dw_hbm, dw_ref, small_sems.at[1]),
    ]
    for small in smalls:
        small.start()
    for small in smalls:
        small.wait()
    classes = lax.broadcasted_iota(jnp.int32, (n, C), 1).astype(jnp.float32)
    spread = jnp.broadcast_to(lab_ref[...].astype(jnp.float32), (C, n)).T
    all_weight = jnp.broadcast_to(dw_ref[...], (C, n)).T
    all_signs = jnp.where(spread == classes, 1.0, -1.0)
    start = logistic_prox(jnp.zeros((n, C), jnp.float32), all_signs, all_weight)
    signs_ref[...] = all_signs
    weight_ref[...] = all_weight
    own = pl.ds(pl.multiple_of(fme * share, share), share)
    signs = signs_ref[own, :]
    weight = weight_ref[own, :]
    margins = logistic_prox(jnp.zeros((share, C), jnp.float32), signs, weight)
    duals = jnp.zeros((share, C), jnp.float32)
    rho = jnp.ones((1, 1), jnp.float32)
    inv = inv_ref[...]
    target = start / num_feat
    residue = target
    growth = None

    groups = wstep.shape[2]
    rows_per = wide // groups

    def w_copy(direction, src, s, peer):
        return [
            remote(
                ref.at[src, s], ref.at[src, s],
                w_sems.at[direction, k, 0, src, s], w_sems.at[direction, k, 1, src, s], "doc", peer,
            )
            for k, ref in enumerate((wcode, wstep))
        ]

    def w_write(src, s):
        for g in range(groups):
            first = pl.multiple_of(src * chunk + s * wide + g * rows_per, rows_per)
            piece = wcode[src, s, g * rows_per : (g + 1) * rows_per, :]
            w_ref[pl.ds(first, rows_per), :] = decode(piece, wstep[src, s, g])

    for step in range(ITERS):
        last = step + 1 == ITERS
        answer = three_dot(inv, three_right(residue))
        applied = residue - answer
        new_part = target - answer
        solved[step, me], solved_step[step, me] = encode(answer)
        part[step] = new_part
        for peer in ch_s.peers():
            ch_s.send(2 * step, peer, solved.at[step, me], solved.at[step, me])
            ch_s.send(2 * step + 1, peer, solved_step.at[step, me], solved_step.at[step, me])
        for peer in ch_y.peers():
            rows = pl.ds(pl.multiple_of(peer * share, share), share)
            ch_y.send(step, peer, part.at[step, rows, :], yrecv.at[step, fme])
        yrecv[step, fme] = part[step, own, :]
        for peer in ch_y.peers():
            ch_y.arrived(step, peer, yrecv.at[step, peer])
        sums = yrecv[step, 0]
        for k in range(1, num_feat):
            sums += yrecv[step, k]
        old_margins = margins
        margins = logistic_prox(sums + duals, signs, weight / rho)
        duals = duals + sums - margins
        cbuf[step, fme, 0] = margins if last else (margins - sums) / num_feat
        cbuf[step, fme, 1] = duals / num_feat
        for peer in ch_c.peers():
            ch_c.send(step, peer, cbuf.at[step, fme], cbuf.at[step, fme])
        for peer in ch_s.peers():
            ch_s.arrived(2 * step, peer, solved.at[step, peer])
            ch_s.arrived(2 * step + 1, peer, solved_step.at[step, peer])
        everything = jnp.concatenate(
            split(decode(solved[step], solved_step[step]).reshape(num_doc * n, C)), axis=1
        )
        limit = shrink_level / (rho * num_doc)
        if not last:
            gap = fold((sums - margins) ** 2) if share > 8 else (sums - margins) ** 2
            shift = (
                fold((margins - old_margins) ** 2) if share > 8 else (margins - old_margins) ** 2
            )
            if step == 0:
                d_answer, d_applied = answer, applied
            else:
                d_answer = answer - last_answer / growth
                d_applied = applied - last_applied / growth
            primal = gap + fold(d_answer * d_applied)
            dual = shift
        for s in range(subs):
            rows = slice(s * wide, (s + 1) * wide)
            lift = split_dot(featt_ref[0, rows, :], featt_ref[1, rows, :], everything)
            if step == 0:
                fresh = shrink_values(lift / num_doc, limit)
                move = -fresh
                d_move, d_lift = move, lift
            else:
                old = z[rows, :]
                fresh = shrink_values(old + lift / num_doc, limit)
                if not last:
                    move = old - fresh
                    d_move = move - lastmove[rows, :] / growth
                    d_lift = lift - lastlift[rows, :] / growth
            if last:
                for g in range(groups):
                    piece = slice(g * rows_per, (g + 1) * rows_per)
                    wcode[me, s, piece, :], wstep[me, s, g] = encode(num_feat * fresh[piece])

                @pl.when(me + 1 < num_doc)
                def _(s=s):
                    for copy in w_copy(0, me, s, me + 1):
                        copy.start()

                @pl.when(me >= 1)
                def _(s=s):
                    for copy in w_copy(1, me, s, me - 1):
                        copy.start()

                w_write(me, s)
            else:
                z[rows, :] = fresh
                lastmove[rows, :] = move
                lastlift[rows, :] = lift
                primal += fold(num_doc * d_move * d_move + 2.0 * d_move * d_lift)
                dual += num_doc * fold(move * move)
        if last:
            break
        sc1[step, me, 0] = primal
        sc1[step, me, 1] = dual
        for peer in ch_1.peers():
            ch_1.send(step, peer, sc1.at[step, me], sc1.at[step, me])
        weights = jnp.concatenate(split(z[...]), axis=1)
        for k in range(1, num_doc + 1):
            peer = lax.rem(me + k, num_doc)
            block = pl.ds(pl.multiple_of(peer * n, n), n)
            product = split_dot(feat_ref[0, block, :], feat_ref[1, block, :], weights)
            if k < num_doc:
                psend[step, k - 1], psend_step[step, k - 1] = encode(product)
                ch_p.send(2 * step, peer, psend.at[step, k - 1], precv.at[step, me])
                ch_p.send(2 * step + 1, peer, psend_step.at[step, k - 1], precv_step.at[step, me])
        for peer in ch_1.peers():
            ch_1.arrived(step, peer, sc1.at[step, peer])
        both = sc1[step, 0]
        for i in range(1, num_doc):
            both += sc1[step, i]
        sc2[step, fme] = both
        for peer in ch_2.peers():
            ch_2.send(step, peer, sc2.at[step, fme], sc2.at[step, fme])
        for peer in ch_2.peers():
            ch_2.arrived(step, peer, sc2.at[step, peer])
        both = sc2[step, 0]
        for k in range(1, num_feat):
            both += sc2[step, k]
        primal = jnp.maximum(total(both[0]), 0.0)
        dual = total(both[1])
        last_answer, last_applied = answer, applied
        for peer in ch_c.peers():
            ch_c.arrived(step, peer, cbuf.at[step, peer])
        growth = jnp.sqrt(
            jnp.sqrt((primal + ratio_floor) / (rho * rho * dual + ratio_floor))
        )
        rho = rho * growth
        duals = duals / growth
        fixed = cbuf[step, :, 0].reshape(n, C) - cbuf[step, :, 1].reshape(n, C) / growth
        target = new_part + fixed
        for peer in ch_p.peers():
            ch_p.arrived(2 * step, peer, precv.at[step, peer])
            ch_p.arrived(2 * step + 1, peer, precv_step.at[step, peer])
            product += decode(precv[step, peer], precv_step[step, peer])
        previous = jnp.zeros((n, C), jnp.float32) if step == 0 else old_product
        residue = target - (product - (previous - product + applied) / growth)
        old_product = product
    for hop in range(1, num_doc):
        for s in range(subs):

            @pl.when(me >= hop)
            def _(hop=hop, s=s):
                for copy in w_copy(0, me - hop, s, me):
                    copy.wait_recv()

                @pl.when(me + 1 < num_doc)
                def _():
                    for copy in w_copy(0, me - hop, s, me + 1):
                        copy.start()

                w_write(me - hop, s)

            @pl.when(me + hop < num_doc)
            def _(hop=hop, s=s):
                for copy in w_copy(1, me + hop, s, me):
                    copy.wait_recv()

                @pl.when(me >= 1)
                def _():
                    for copy in w_copy(1, me + hop, s, me - 1):
                        copy.start()

                w_write(me + hop, s)

    for peer in ch_c.peers():
        ch_c.arrived(ITERS - 1, peer, cbuf.at[ITERS - 1, peer])
    m_ref[...] = cbuf[ITERS - 1, :, 0].reshape(n, C)
    for hop in range(num_doc):
        for s in range(subs):

            @pl.when((me >= hop) & (me + 1 < num_doc))
            def _(hop=hop, s=s):
                for copy in w_copy(0, me - hop, s, me + 1):
                    copy.wait_send()

            @pl.when((me + hop < num_doc) & (me >= 1))
            def _(hop=hop, s=s):
                for copy in w_copy(1, me + hop, s, me - 1):
                    copy.wait_send()

    for channel in (ch_s, ch_y, ch_c, ch_p, ch_1, ch_2):
        channel.drain()


def whole_kernel(
    num_doc, num_feat, subs, scale,
    docs_ref, dir_ref, phase_hbm, amp_hbm, lab_ref, dw_ref,
    m_ref, w_ref,
    feat_ref, featt_ref, gram_ref, inv_ref,
    *scratch,
):
    build_kernel(
        num_doc, num_feat, subs, scale,
        docs_ref, dir_ref, phase_hbm, amp_hbm, feat_ref, featt_ref, gram_ref, *scratch[:13],
    )
    inv_ref[...] = three_left(invert(gram_ref[...]))
    admm_kernel(
        num_doc, num_feat, subs,
        feat_ref, featt_ref, inv_ref, lab_ref, dw_ref, m_ref, w_ref, *scratch[13:],
    )


def hand_over(margins_ref, weights_ref, m_ref, w_ref, sems):
    copies = [
        pltpu.make_async_copy(margins_ref, m_ref, sems.at[0]),
        pltpu.make_async_copy(weights_ref, w_ref, sems.at[1]),
    ]
    for copy in copies:
        copy.start()
    for copy in copies:
        copy.wait()


def per_device(documents, directions, phase, amplitude, doc_weight, labels):
    n, local_inputs = documents.shape
    input_rows, width_tile = directions.shape
    num_feat = lax.axis_size("feat")
    num_doc = lax.axis_size("doc")
    chunk = width_tile // num_doc
    subs = max(1, min(4, chunk // 128))
    share = n // num_feat
    f32, bf16 = jnp.float32, jnp.bfloat16
    vmem = pl.BlockSpec(memory_space=pltpu.VMEM)
    dma = pltpu.SemaphoreType.DMA
    shape = jax.ShapeDtypeStruct
    rounds = ITERS - 1
    anywhere = pl.BlockSpec(memory_space=pl.ANY)
    groups = max(1, chunk // subs // n)
    operands = (
        documents.T,
        directions,
        phase.reshape(num_doc, 1, chunk),
        amplitude.reshape(num_doc, 1, chunk),
        labels.reshape(1, n),
        doc_weight.reshape(1, n),
    )
    margins, weights = pl.pallas_call(
        functools.partial(
            whole_kernel, num_doc, num_feat, subs, (2.0 / width_tile) ** 0.5
        ),
        out_shape=(shape((n, C), f32), shape((width_tile, C), f32)),
        in_specs=[anywhere] * 6,
        out_specs=(vmem, vmem),
        scratch_shapes=[
            pltpu.VMEM((2, num_doc * n, chunk), bf16),
            pltpu.VMEM((2, chunk, num_doc * n), bf16),
            pltpu.VMEM((n, n), f32),
            pltpu.VMEM((n, 3 * n), bf16),
            pltpu.VMEM((num_feat, num_doc, local_inputs, n), bf16),
            pltpu.VMEM((1, chunk), f32),
            pltpu.VMEM((1, chunk), f32),
            pltpu.VMEM((num_doc, input_rows, chunk), bf16),
            pltpu.VMEM((num_doc, n, 2 * n), f32),
            pltpu.VMEM((num_doc, n // 2 + 8, n), f32),
            pltpu.VMEM((num_doc, n // 2 + 8, n), f32),
            dma((2, 1, num_feat)),
            dma((2, 1, num_doc)),
            dma((2, subs, num_doc)),
            dma((2, 1, num_doc)),
            dma,
            dma((3,)),
            pltpu.VMEM((1, n), jnp.int32),
            pltpu.VMEM((1, n), f32),
            dma((2,)),
            pltpu.VMEM((ITERS, num_doc, n, C), jnp.int16),
            pltpu.VMEM((ITERS, num_doc, 1, C), f32),
            pltpu.VMEM((ITERS, n, C), f32),
            pltpu.VMEM((ITERS, num_feat, share, C), f32),
            pltpu.VMEM((ITERS, num_feat, 2, share, C), f32),
            pltpu.VMEM((rounds, num_doc, n, C), jnp.int16),
            pltpu.VMEM((rounds, num_doc, 1, C), f32),
            pltpu.VMEM((rounds, num_doc, n, C), jnp.int16),
            pltpu.VMEM((rounds, num_doc, 1, C), f32),
            pltpu.VMEM((rounds, num_doc, 2, 8, C), f32),
            pltpu.VMEM((rounds, num_feat, 2, 8, C), f32),
            pltpu.VMEM((chunk, C), f32),
            pltpu.VMEM((chunk, C), f32),
            pltpu.VMEM((chunk, C), f32),
            pltpu.VMEM((n, C), f32),
            pltpu.VMEM((n, C), f32),
            pltpu.VMEM((num_doc, subs, chunk // subs, C), jnp.int16),
            pltpu.VMEM((num_doc, subs, groups, 1, C), f32),
            dma((2, 2 * ITERS, num_doc)),
            dma((2, ITERS, num_feat)),
            dma((2, ITERS, num_feat)),
            dma((2, 2 * rounds, num_doc)),
            dma((2, rounds, num_doc)),
            dma((2, rounds, num_feat)),
            dma((2, 2, 2, num_doc, subs)),
        ],
        compiler_params=pltpu.CompilerParams(
            collective_id=0, has_side_effects=True, vmem_limit_bytes=48 * 1024 * 1024
        ),
        name="admm",
    )(*[pltpu.with_memory_space_constraint(operand, pltpu.HBM) for operand in operands])
    return pl.pallas_call(
        hand_over,
        out_shape=(shape((n, C), f32), shape((width_tile, C), f32)),
        in_specs=[anywhere] * 2,
        out_specs=(anywhere,) * 2,
        scratch_shapes=[dma((2,))],
        compiler_params=pltpu.CompilerParams(vmem_limit_bytes=1024 * 1024),
        name="hand_over",
    )(margins, weights)


def solution(mesh):
    in_specs = (P("doc", "feat"), P("doc", "feat"), P("feat"), P("feat"), P("doc"), P("doc"))
    out_specs = (P("doc", None), P("feat", None))
    return jax.shard_map(
        per_device, mesh=mesh, in_specs=in_specs, out_specs=out_specs, check_vma=False
    )
```

```python
import functools

import jax
import jax.numpy as jnp
from jax import lax
from jax.experimental import pallas as pl
from jax.experimental.pallas import tpu as pltpu
from jax.sharding import PartitionSpec as P

C = 128
ITERS = 3
NEWTON = 3
LEVELS = 32767.0
INVERSE_STEPS = 7
WINDOW = 2
DIR_SUBS = 2
HI = lax.Precision.HIGHEST
MESH = pl.DeviceIdType.MESH

shrink_level = 0.1
ratio_floor = 1e-06


def logistic_prox(target, signs, weight_ratio):
    current = target
    for newton_step in range(NEWTON):
        chance = 1.0 / (1.0 + jnp.exp(signs * current))
        gradient = current - target - weight_ratio * signs * chance
        current = current - gradient / (1.0 + weight_ratio * chance * (1.0 - chance))
    return current


def shrink_values(target, limit):
    return target - jnp.minimum(jnp.maximum(target, -limit), limit)


def cosine(angle):
    turns = jnp.floor(angle * 0.3183098861837907 + 0.5)
    rest = angle - turns * 3.140625
    rest = rest - turns * 9.67502593994140625e-4
    rest = rest - turns * 1.509957990978376432e-7
    odd = turns - 2.0 * jnp.floor(turns * 0.5)
    sq = rest * rest
    poly = 2.08767569878681e-9
    poly = poly * sq - 2.755731922398589e-7
    poly = poly * sq + 2.48015873015873e-5
    poly = poly * sq - 1.388888888888889e-3
    poly = poly * sq + 4.1666666666666664e-2
    poly = poly * sq - 0.5
    poly = poly * sq + 1.0
    return poly * (1.0 - 2.0 * odd)


def split(values):
    high = values.astype(jnp.bfloat16)
    return high, (values - high.astype(jnp.float32)).astype(jnp.bfloat16)


def split_dot(high, low, pair):
    both = jnp.dot(high, pair, preferred_element_type=jnp.float32)
    rest = jnp.dot(low, pair[:, :C], preferred_element_type=jnp.float32)
    return both[:, :C] + (both[:, C:] + rest)


def encode(values):
    largest = jnp.max(jnp.abs(values), axis=0, keepdims=True)
    steps = jnp.where(largest > 0.0, LEVELS / largest, 0.0)
    codes = jnp.floor(values * steps + 0.5).astype(jnp.int32).astype(jnp.int16)
    return codes, largest * (1.0 / LEVELS)


def decode(codes, steps):
    return codes.astype(jnp.int32).astype(jnp.float32) * steps


def remote(src, dst, send_sem, recv_sem, axis, peer):
    return pltpu.make_async_remote_copy(
        src_ref=src,
        dst_ref=dst,
        send_sem=send_sem,
        recv_sem=recv_sem,
        device_id={axis: peer},
        device_id_type=MESH,
    )


def greet(num_doc, num_feat):
    barrier = pltpu.get_barrier_semaphore()
    for axis, size in (("doc", num_doc), ("feat", num_feat)):
        me = lax.axis_index(axis)
        for k in range(1, size):
            pl.semaphore_signal(
                barrier, inc=1, device_id={axis: lax.rem(me + k, size)}, device_id_type=MESH
            )
    pl.semaphore_wait(barrier, num_doc + num_feat - 2)


class Channel:
    def __init__(self, sems, axis, size):
        self.sems, self.axis, self.size = sems, axis, size
        self.me = lax.axis_index(axis)
        self.pending = []

    def peers(self):
        return [lax.rem(self.me + k, self.size) for k in range(1, self.size)]

    def send(self, slot, peer, src, dst):
        copy = remote(
            src, dst, self.sems.at[0, slot, peer], self.sems.at[1, slot, self.me], self.axis, peer
        )
        copy.start()
        self.pending.append(copy)

    def arrived(self, slot, peer, ref):
        remote(
            ref, ref, self.sems.at[0, slot, peer], self.sems.at[1, slot, peer], self.axis, peer
        ).wait_recv()

    def drain(self, count=None):
        count = len(self.pending) if count is None else count
        for copy in self.pending[:count]:
            copy.wait_send()
        self.pending = self.pending[count:]


def build_kernel(
    num_doc, num_feat, subs, scale,
    docs_ref, dir_ref, phase_hbm, amp_hbm,
    feat_ref, featt_ref, gram_ref,
    dpart, phase_ref, amp_ref, dirs, gsum, gsend, grecv,
    part_sems, row_sems, dir_sems, gram_sems, local_sem, table_sems,
):
    n = docs_ref.shape[1]
    chunk = dirs.shape[2]
    wide = chunk // subs
    me = lax.axis_index("doc")
    fme = lax.axis_index("feat")
    tables = [
        pltpu.make_async_copy(docs_ref, dpart.at[fme, me], table_sems.at[2]),
        pltpu.make_async_copy(phase_hbm.at[me], phase_ref, table_sems.at[0]),
        pltpu.make_async_copy(amp_hbm.at[me], amp_ref, table_sems.at[1]),
    ]
    for table in tables:
        table.start()
    local = pltpu.make_async_copy(
        dir_ref.at[:, pl.ds(pl.multiple_of(me * chunk, chunk), chunk)], dirs.at[me], local_sem
    )
    local.start()
    greet(num_doc, num_feat)
    ch_part = Channel(part_sems, "feat", num_feat)
    ch_row = Channel(row_sems, "doc", num_doc)
    ch_dir = Channel(dir_sems, "doc", num_doc)
    ch_gram = Channel(gram_sems, "doc", num_doc)
    for peer in ch_row.peers():
        ch_row.send(0, peer, docs_ref, dpart.at[fme, me])
    def send_dirs(s):
        for peer in ch_dir.peers():
            cols = pl.ds(pl.multiple_of(peer * chunk + s * wide, wide), wide)
            ch_dir.send(
                s, peer, dir_ref.at[:, cols], dirs.at[me, :, pl.ds(s * wide, wide)]
            )

    for s in range(min(WINDOW, subs)):
        send_dirs(s)
    tables[0].wait()
    for peer in ch_row.peers():
        ch_row.arrived(0, peer, dpart.at[fme, peer])
    for peer in ch_part.peers():
        ch_part.send(0, peer, dpart.at[fme], dpart.at[fme])
    for peer in ch_part.peers():
        ch_part.arrived(0, peer, dpart.at[peer])
    inputs = num_feat * docs_ref.shape[0]
    full = jnp.concatenate([dpart[:, i].reshape(inputs, n).T for i in range(num_doc)], axis=0)
    local.wait()
    for table in tables[1:]:
        table.wait()
    phase = phase_ref[...]
    amp = scale * amp_ref[...]
    for s in range(subs):
        cols = slice(s * wide, (s + 1) * wide)
        for peer in ch_dir.peers():
            ch_dir.arrived(s, peer, dirs.at[peer, :, pl.ds(s * wide, wide)])
        if s + WINDOW < subs:
            ch_dir.drain(num_doc - 1)
            send_dirs(s + WINDOW)
        piece = dirs[:, :, cols].reshape(full.shape[1], wide)
        angles = jnp.dot(full, piece, preferred_element_type=jnp.float32)
        feats = amp[:, cols] * cosine(angles + phase[:, cols])
        high, low = split(feats)
        feat_ref[0, :, cols], feat_ref[1, :, cols] = high, low
        for i in range(num_doc):
            block = slice(i * n, (i + 1) * n)
            term = lax.dot_general(
                high[block],
                jnp.concatenate([high[block], low[block]], axis=0),
                (((1,), (1,)), ((), ())),
                preferred_element_type=jnp.float32,
            )
            if s == 0:
                gsum[i] = term
            else:
                gsum[i] += term
        featt_ref[0, cols, :], featt_ref[1, cols, :] = split(feats.T)
    for k in range(1, num_doc + 1):
        peer = lax.rem(me + k, num_doc)
        mixed = gsum[peer, :, n:]
        gsend[peer] = pack_symmetric(gsum[peer, :, :n] + (mixed + mixed.T))
        if k < num_doc:
            ch_gram.send(0, peer, gsend.at[peer], grecv.at[me])
    total = gsend[me]
    for peer in ch_gram.peers():
        ch_gram.arrived(0, peer, grecv.at[peer])
        total += grecv[peer]
    gram_ref[...] = unpack_symmetric(total)
    for channel in (ch_part, ch_row, ch_dir, ch_gram):
        channel.drain()


def pack_symmetric(values):
    half = values.shape[0] // 2
    rows = lax.broadcasted_iota(jnp.int32, (half, 2 * half), 0)
    lanes = lax.broadcasted_iota(jnp.int32, (half, 2 * half), 1)
    top, bottom = values[:half], values[half:]
    both = jnp.where(lanes <= rows + half, bottom, pltpu.roll(top, half, 1))
    diagonal = jnp.sum(jnp.where(rows == lanes, top, 0.0), axis=0, keepdims=True)
    return jnp.concatenate([both, jnp.broadcast_to(diagonal, (8, 2 * half))], axis=0)


def unpack_symmetric(packed):
    half = packed.shape[0] - 8
    rows = lax.broadcasted_iota(jnp.int32, (half, 2 * half), 0)
    lanes = lax.broadcasted_iota(jnp.int32, (half, 2 * half), 1)
    both, diagonal = packed[:half], packed[half : half + 1]
    flipped = jnp.concatenate([both, both], axis=0).T
    bottom = jnp.where(lanes <= rows + half, both, flipped[half:])
    corner = jnp.where(lanes > rows, pltpu.roll(both, half, 1), flipped[half:])
    corner = jnp.where(lanes == rows, diagonal, corner)
    return jnp.concatenate([jnp.where(lanes >= half, flipped[:half], corner), bottom], axis=0)


def three_left(values):
    high, low = split(values)
    return jnp.concatenate([high, high, low], axis=1)


def three_right(values):
    high, low = split(values)
    return jnp.concatenate([high, low, high], axis=0)


def three_dot(left, right):
    return jnp.dot(left, right, preferred_element_type=jnp.float32)


def invert(gram):
    n = gram.shape[0]
    rows = lax.broadcasted_iota(jnp.int32, (n, n), 0)
    lanes = lax.broadcasted_iota(jnp.int32, (n, n), 1)
    eye = jnp.where(rows == lanes, 1.0, 0.0)
    matrix = gram + eye
    bound = jnp.max(jnp.sum(jnp.abs(matrix), axis=0, keepdims=True), axis=1, keepdims=True)
    first = 2.0 / (1.0 + bound)
    error = (bound - 1.0) / (bound + 1.0)
    near = first * matrix
    guess = first * eye
    for k in range(INVERSE_STEPS):
        scale = 2.0 / (2.0 - error * error)
        error = 0.5 * error * error * scale
        if k == 0:
            moved = jnp.concatenate([first * near, three_dot(three_left(near), three_right(near))], axis=1)
        else:
            moved = three_dot(
                three_left(near), three_right(jnp.concatenate([guess, near], axis=1))
            )
        guess = scale * (2.0 * guess - moved[:, :n])
        near = scale * (2.0 * near - moved[:, n:])
    missing = eye - jnp.dot(matrix, guess, precision=HI)
    return guess + three_dot(three_left(guess), three_right(missing))


def fold(values):
    return jnp.sum(values.reshape(values.shape[0] // 8, 8, values.shape[1]), axis=0)


def admm_kernel(
    num_doc, num_feat, subs,
    feat_ref, featt_ref, inv_ref, lab_hbm, dw_hbm,
    m_ref, w_ref, lab_ref, dw_ref, small_sems,
    solved, solved_step, part, yrecv, cbuf, psend, psend_step, precv, precv_step,
    norms, z, lastmove, lastlift, signs_ref, weight_ref, wcode, wstep,
    s_sems, y_sems, c_sems, p_sems, norm_sems, w_sems,
):
    n = inv_ref.shape[0]
    chunk = z.shape[0]
    share = n // num_feat
    wide = chunk // subs
    me = lax.axis_index("doc")
    fme = lax.axis_index("feat")
    ch_s = Channel(s_sems, "doc", num_doc)
    ch_y = Channel(y_sems, "feat", num_feat)
    ch_c = Channel(c_sems, "feat", num_feat)
    ch_p = Channel(p_sems, "doc", num_doc)
    smalls = [
        pltpu.make_async_copy(lab_hbm, lab_ref, small_sems.at[0]),
        pltpu.make_async_copy(dw_hbm, dw_ref, small_sems.at[1]),
    ]
    for small in smalls:
        small.start()
    for small in smalls:
        small.wait()
    classes = lax.broadcasted_iota(jnp.int32, (n, C), 1).astype(jnp.float32)
    spread = jnp.broadcast_to(lab_ref[...].astype(jnp.float32), (C, n)).T
    all_weight = jnp.broadcast_to(dw_ref[...], (C, n)).T
    all_signs = jnp.where(spread == classes, 1.0, -1.0)
    start = logistic_prox(jnp.zeros((n, C), jnp.float32), all_signs, all_weight)
    signs_ref[...] = all_signs
    weight_ref[...] = all_weight
    own = pl.ds(pl.multiple_of(fme * share, share), share)
    signs = signs_ref[own, :]
    weight = weight_ref[own, :]
    margins = logistic_prox(jnp.zeros((share, C), jnp.float32), signs, weight)
    duals = jnp.zeros((share, C), jnp.float32)
    rho = jnp.ones((1, 1), jnp.float32)
    inv = inv_ref[...]
    target = start / num_feat
    residue = target
    growth = None

    mine = me * num_feat + fme
    others = [
        (lax.rem(me + i, num_doc), lax.rem(fme + j, num_feat))
        for i in range(num_doc)
        for j in range(num_feat)
        if i or j
    ]
    norm_copies = []

    def norm_copy(step, source, target):
        row = norms.at[step, source]
        return pltpu.make_async_remote_copy(
            src_ref=row,
            dst_ref=row,
            send_sem=norm_sems.at[0, step, target[0] * num_feat + target[1]],
            recv_sem=norm_sems.at[1, step, source],
            device_id={"doc": target[0], "feat": target[1]},
            device_id_type=MESH,
        )

    groups = wstep.shape[2]
    rows_per = wide // groups

    def w_copy(direction, src, s, peer):
        return [
            remote(
                ref.at[src, s], ref.at[src, s],
                w_sems.at[direction, k, 0, src, s], w_sems.at[direction, k, 1, src, s], "doc", peer,
            )
            for k, ref in enumerate((wcode, wstep))
        ]

    def w_write(src, s):
        for g in range(groups):
            first = pl.multiple_of(src * chunk + s * wide + g * rows_per, rows_per)
            piece = wcode[src, s, g * rows_per : (g + 1) * rows_per, :]
            w_ref[pl.ds(first, rows_per), :] = decode(piece, wstep[src, s, g])

    def send_margins(step):
        for peer in ch_c.peers():
            ch_c.send(step, peer, cbuf.at[step, fme], cbuf.at[step, fme])

    for step in range(ITERS):
        last = step + 1 == ITERS
        if step == 0:
            answer = three_dot(inv, three_right(residue))
        applied = residue - answer
        new_part = target - answer
        solved[step, me], solved_step[step, me] = encode(answer)
        part[step] = new_part
        for peer in ch_s.peers():
            ch_s.send(2 * step, peer, solved.at[step, me], solved.at[step, me])
            ch_s.send(2 * step + 1, peer, solved_step.at[step, me], solved_step.at[step, me])
        for peer in ch_y.peers():
            rows = pl.ds(pl.multiple_of(peer * share, share), share)
            ch_y.send(step, peer, part.at[step, rows, :], yrecv.at[step, fme])
        yrecv[step, fme] = part[step, own, :]
        for peer in ch_y.peers():
            ch_y.arrived(step, peer, yrecv.at[step, peer])
        sums = yrecv[step, 0]
        for k in range(1, num_feat):
            sums += yrecv[step, k]
        old_margins = margins
        margins = logistic_prox(sums + duals, signs, weight / rho)
        duals = duals + sums - margins
        cbuf[step, fme, 0] = margins if last else (margins - sums) / num_feat
        cbuf[step, fme, 1] = duals / num_feat
        if last:
            send_margins(step)
        for peer in ch_s.peers():
            ch_s.arrived(2 * step, peer, solved.at[step, peer])
            ch_s.arrived(2 * step + 1, peer, solved_step.at[step, peer])
        everything = jnp.concatenate(
            split(decode(solved[step], solved_step[step]).reshape(num_doc * n, C)), axis=1
        )
        limit = shrink_level / (rho * num_doc)
        if not last:
            gap = fold((sums - margins) ** 2) if share > 8 else (sums - margins) ** 2
            shift = (
                fold((margins - old_margins) ** 2) if share > 8 else (margins - old_margins) ** 2
            )
            if step == 0:
                d_answer, d_applied = answer, applied
            else:
                d_answer = answer - last_answer / growth
                d_applied = applied - last_applied / growth
            primal = gap + fold(d_answer * d_applied)
            dual = shift
        for s in range(subs):
            rows = slice(s * wide, (s + 1) * wide)
            lift = split_dot(featt_ref[0, rows, :], featt_ref[1, rows, :], everything)
            if step == 0:
                fresh = shrink_values(lift / num_doc, limit)
                move = -fresh
                d_move, d_lift = move, lift
            else:
                old = z[rows, :]
                fresh = shrink_values(old + lift / num_doc, limit)
                if not last:
                    move = old - fresh
                    d_move = move - lastmove[rows, :] / growth
                    d_lift = lift - lastlift[rows, :] / growth
            if last:
                for g in range(groups):
                    piece = slice(g * rows_per, (g + 1) * rows_per)
                    wcode[me, s, piece, :], wstep[me, s, g] = encode(num_feat * fresh[piece])

                @pl.when(me + 1 < num_doc)
                def _(s=s):
                    for copy in w_copy(0, me, s, me + 1):
                        copy.start()

                @pl.when(me >= 1)
                def _(s=s):
                    for copy in w_copy(1, me, s, me - 1):
                        copy.start()

                w_write(me, s)
            else:
                z[rows, :] = fresh
                lastmove[rows, :] = move
                lastlift[rows, :] = lift
                primal += fold(num_doc * d_move * d_move + 2.0 * d_move * d_lift)
                dual += num_doc * fold(move * move)
        if last:
            break
        send_margins(step)
        norms[step, mine, 0:1] = jnp.sum(primal, axis=0, keepdims=True)
        norms[step, mine, 1:2] = jnp.sum(dual, axis=0, keepdims=True)
        weights = jnp.concatenate(split(z[...]), axis=1)
        for k in range(1, num_doc + 1):
            peer = lax.rem(me + k, num_doc)
            block = pl.ds(pl.multiple_of(peer * n, n), n)
            product = split_dot(feat_ref[0, block, :], feat_ref[1, block, :], weights)
            if k < num_doc:
                psend[step, k - 1], psend_step[step, k - 1] = encode(product)
                ch_p.send(2 * step, peer, psend.at[step, k - 1], precv.at[step, me])
                ch_p.send(2 * step + 1, peer, psend_step.at[step, k - 1], precv_step.at[step, me])
        for target in others:
            copy = norm_copy(step, mine, target)
            copy.start()
            norm_copies.append(copy)
        last_answer, last_applied = answer, applied
        for peer in ch_c.peers():
            ch_c.arrived(step, peer, cbuf.at[step, peer])
        margins_part = cbuf[step, :, 0].reshape(n, C)
        duals_part = cbuf[step, :, 1].reshape(n, C)
        for peer in ch_p.peers():
            ch_p.arrived(2 * step, peer, precv.at[step, peer])
            ch_p.arrived(2 * step + 1, peer, precv_step.at[step, peer])
            product += decode(precv[step, peer], precv_step[step, peer])
        kept = new_part + margins_part - product
        shrunk = applied - product - duals_part if step == 0 else (
            old_product - product + applied - duals_part
        )
        old_product = product
        both = three_dot(inv, three_right(jnp.concatenate([kept, shrunk], axis=1)))
        for source in others:
            norm_copy(step, source[0] * num_feat + source[1], source).wait_recv()
        sums_of = jnp.sum(jnp.sum(norms[step], axis=0), axis=1, keepdims=True)
        primal = jnp.maximum(sums_of[0:1], 0.0)
        dual = sums_of[1:2]
        growth = jnp.sqrt(
            jnp.sqrt((primal + ratio_floor) / (rho * rho * dual + ratio_floor))
        )
        rho = rho * growth
        shrink = 1.0 / growth
        duals = duals * shrink
        target = new_part + margins_part - duals_part * shrink
        residue = kept + shrunk * shrink
        answer = both[:, :C] + both[:, C:] * shrink
    for hop in range(1, num_doc):
        for s in range(subs):

            @pl.when(me >= hop)
            def _(hop=hop, s=s):
                for copy in w_copy(0, me - hop, s, me):
                    copy.wait_recv()

                @pl.when(me + 1 < num_doc)
                def _():
                    for copy in w_copy(0, me - hop, s, me + 1):
                        copy.start()

                w_write(me - hop, s)

            @pl.when(me + hop < num_doc)
            def _(hop=hop, s=s):
                for copy in w_copy(1, me + hop, s, me):
                    copy.wait_recv()

                @pl.when(me >= 1)
                def _():
                    for copy in w_copy(1, me + hop, s, me - 1):
                        copy.start()

                w_write(me + hop, s)

    for peer in ch_c.peers():
        ch_c.arrived(ITERS - 1, peer, cbuf.at[ITERS - 1, peer])
    m_ref[...] = cbuf[ITERS - 1, :, 0].reshape(n, C)
    for hop in range(num_doc):
        for s in range(subs):

            @pl.when((me >= hop) & (me + 1 < num_doc))
            def _(hop=hop, s=s):
                for copy in w_copy(0, me - hop, s, me + 1):
                    copy.wait_send()

            @pl.when((me + hop < num_doc) & (me >= 1))
            def _(hop=hop, s=s):
                for copy in w_copy(1, me + hop, s, me - 1):
                    copy.wait_send()

    for channel in (ch_s, ch_y, ch_c, ch_p):
        channel.drain()
    for copy in norm_copies:
        copy.wait_send()


def whole_kernel(
    num_doc, num_feat, subs, dir_subs, scale,
    docs_ref, dir_ref, phase_hbm, amp_hbm, lab_ref, dw_ref,
    m_ref, w_ref,
    feat_ref, featt_ref, gram_ref, inv_ref,
    *scratch,
):
    build_kernel(
        num_doc, num_feat, dir_subs, scale,
        docs_ref, dir_ref, phase_hbm, amp_hbm, feat_ref, featt_ref, gram_ref, *scratch[:13],
    )
    inv_ref[...] = three_left(invert(gram_ref[...]))
    admm_kernel(
        num_doc, num_feat, subs,
        feat_ref, featt_ref, inv_ref, lab_ref, dw_ref, m_ref, w_ref, *scratch[13:],
    )


def hand_over(margins_ref, weights_ref, m_ref, w_ref, sems):
    copies = [
        pltpu.make_async_copy(margins_ref, m_ref, sems.at[0]),
        pltpu.make_async_copy(weights_ref, w_ref, sems.at[1]),
    ]
    for copy in copies:
        copy.start()
    for copy in copies:
        copy.wait()


def per_device(documents, directions, phase, amplitude, doc_weight, labels):
    n, local_inputs = documents.shape
    input_rows, width_tile = directions.shape
    num_feat = lax.axis_size("feat")
    num_doc = lax.axis_size("doc")
    chunk = width_tile // num_doc
    subs = max(1, min(4, chunk // 128))
    dir_subs = max(1, min(DIR_SUBS, chunk // 128))
    share = n // num_feat
    f32, bf16 = jnp.float32, jnp.bfloat16
    vmem = pl.BlockSpec(memory_space=pltpu.VMEM)
    dma = pltpu.SemaphoreType.DMA
    shape = jax.ShapeDtypeStruct
    rounds = ITERS - 1
    anywhere = pl.BlockSpec(memory_space=pl.ANY)
    groups = max(1, chunk // subs // n)
    operands = (
        documents.T,
        directions,
        phase.reshape(num_doc, 1, chunk),
        amplitude.reshape(num_doc, 1, chunk),
        labels.reshape(1, n),
        doc_weight.reshape(1, n),
    )
    margins, weights = pl.pallas_call(
        functools.partial(
            whole_kernel, num_doc, num_feat, subs, dir_subs, (2.0 / width_tile) ** 0.5
        ),
        out_shape=(shape((n, C), f32), shape((width_tile, C), f32)),
        in_specs=[anywhere] * 6,
        out_specs=(vmem, vmem),
        scratch_shapes=[
            pltpu.VMEM((2, num_doc * n, chunk), bf16),
            pltpu.VMEM((2, chunk, num_doc * n), bf16),
            pltpu.VMEM((n, n), f32),
            pltpu.VMEM((n, 3 * n), bf16),
            pltpu.VMEM((num_feat, num_doc, local_inputs, n), bf16),
            pltpu.VMEM((1, chunk), f32),
            pltpu.VMEM((1, chunk), f32),
            pltpu.VMEM((num_doc, input_rows, chunk), bf16),
            pltpu.VMEM((num_doc, n, 2 * n), f32),
            pltpu.VMEM((num_doc, n // 2 + 8, n), f32),
            pltpu.VMEM((num_doc, n // 2 + 8, n), f32),
            dma((2, 1, num_feat)),
            dma((2, 1, num_doc)),
            dma((2, dir_subs, num_doc)),
            dma((2, 1, num_doc)),
            dma,
            dma((3,)),
            pltpu.VMEM((1, n), jnp.int32),
            pltpu.VMEM((1, n), f32),
            dma((2,)),
            pltpu.VMEM((ITERS, num_doc, n, C), jnp.int16),
            pltpu.VMEM((ITERS, num_doc, 1, C), f32),
            pltpu.VMEM((ITERS, n, C), f32),
            pltpu.VMEM((ITERS, num_feat, share, C), f32),
            pltpu.VMEM((ITERS, num_feat, 2, share, C), f32),
            pltpu.VMEM((rounds, num_doc, n, C), jnp.int16),
            pltpu.VMEM((rounds, num_doc, 1, C), f32),
            pltpu.VMEM((rounds, num_doc, n, C), jnp.int16),
            pltpu.VMEM((rounds, num_doc, 1, C), f32),
            pltpu.VMEM((rounds, num_doc * num_feat, 2, C), f32),
            pltpu.VMEM((chunk, C), f32),
            pltpu.VMEM((chunk, C), f32),
            pltpu.VMEM((chunk, C), f32),
            pltpu.VMEM((n, C), f32),
            pltpu.VMEM((n, C), f32),
            pltpu.VMEM((num_doc, subs, chunk // subs, C), jnp.int16),
            pltpu.VMEM((num_doc, subs, groups, 1, C), f32),
            dma((2, 2 * ITERS, num_doc)),
            dma((2, ITERS, num_feat)),
            dma((2, ITERS, num_feat)),
            dma((2, 2 * rounds, num_doc)),
            dma((2, rounds, num_doc * num_feat)),
            dma((2, 2, 2, num_doc, subs)),
        ],
        compiler_params=pltpu.CompilerParams(
            collective_id=0, has_side_effects=True, vmem_limit_bytes=48 * 1024 * 1024
        ),
        name="admm",
    )(*[pltpu.with_memory_space_constraint(operand, pltpu.HBM) for operand in operands])
    return pl.pallas_call(
        hand_over,
        out_shape=(shape((n, C), f32), shape((width_tile, C), f32)),
        in_specs=[anywhere] * 2,
        out_specs=(anywhere,) * 2,
        scratch_shapes=[dma((2,))],
        compiler_params=pltpu.CompilerParams(vmem_limit_bytes=1024 * 1024),
        name="hand_over",
    )(margins, weights)


def solution(mesh):
    in_specs = (P("doc", "feat"), P("doc", "feat"), P("feat"), P("feat"), P("doc"), P("doc"))
    out_specs = (P("doc", None), P("feat", None))
    return jax.shard_map(
        per_device, mesh=mesh, in_specs=in_specs, out_specs=out_specs, check_vma=False
    )
```

```python
import functools

import jax
import jax.numpy as jnp
from jax import lax
from jax.experimental import pallas as pl
from jax.experimental.pallas import tpu as pltpu
from jax.sharding import PartitionSpec as P

C = 128
ITERS = 3
NEWTON = 3
LEVELS = 32767.0
INVERSE_STEPS = 7
WINDOW = 2
DIR_SUBS = 2
HI = lax.Precision.HIGHEST
MESH = pl.DeviceIdType.MESH

shrink_level = 0.1
ratio_floor = 1e-06


def logistic_prox(target, signs, weight_ratio):
    current = target
    for newton_step in range(NEWTON):
        chance = 1.0 / (1.0 + jnp.exp(signs * current))
        gradient = current - target - weight_ratio * signs * chance
        current = current - gradient / (1.0 + weight_ratio * chance * (1.0 - chance))
    return current


def shrink_values(target, limit):
    return target - jnp.minimum(jnp.maximum(target, -limit), limit)


def cosine(angle):
    turns = jnp.floor(angle * 0.3183098861837907 + 0.5)
    rest = angle - turns * 3.140625
    rest = rest - turns * 9.67502593994140625e-4
    rest = rest - turns * 1.509957990978376432e-7
    odd = turns - 2.0 * jnp.floor(turns * 0.5)
    sq = rest * rest
    poly = 2.08767569878681e-9
    poly = poly * sq - 2.755731922398589e-7
    poly = poly * sq + 2.48015873015873e-5
    poly = poly * sq - 1.388888888888889e-3
    poly = poly * sq + 4.1666666666666664e-2
    poly = poly * sq - 0.5
    poly = poly * sq + 1.0
    return poly * (1.0 - 2.0 * odd)


def split(values):
    high = values.astype(jnp.bfloat16)
    return high, (values - high.astype(jnp.float32)).astype(jnp.bfloat16)


def split_dot(high, low, pair):
    both = jnp.dot(high, pair, preferred_element_type=jnp.float32)
    rest = jnp.dot(low, pair[:, :C], preferred_element_type=jnp.float32)
    return both[:, :C] + (both[:, C:] + rest)


def encode(values):
    largest = jnp.max(jnp.abs(values), axis=0, keepdims=True)
    steps = jnp.where(largest > 0.0, LEVELS / largest, 0.0)
    codes = jnp.floor(values * steps + 0.5).astype(jnp.int32).astype(jnp.int16)
    return codes, largest * (1.0 / LEVELS)


def decode(codes, steps):
    return codes.astype(jnp.int32).astype(jnp.float32) * steps


def remote(src, dst, send_sem, recv_sem, axis, peer):
    return pltpu.make_async_remote_copy(
        src_ref=src,
        dst_ref=dst,
        send_sem=send_sem,
        recv_sem=recv_sem,
        device_id={axis: peer},
        device_id_type=MESH,
    )


def greet(num_doc, num_feat):
    barrier = pltpu.get_barrier_semaphore()
    for axis, size in (("doc", num_doc), ("feat", num_feat)):
        me = lax.axis_index(axis)
        for k in range(1, size):
            pl.semaphore_signal(
                barrier, inc=1, device_id={axis: lax.rem(me + k, size)}, device_id_type=MESH
            )
    pl.semaphore_wait(barrier, num_doc + num_feat - 2)


class Channel:
    def __init__(self, sems, axis, size):
        self.sems, self.axis, self.size = sems, axis, size
        self.me = lax.axis_index(axis)
        self.pending = []

    def peers(self):
        return [lax.rem(self.me + k, self.size) for k in range(1, self.size)]

    def send(self, slot, peer, src, dst):
        copy = remote(
            src, dst, self.sems.at[0, slot, peer], self.sems.at[1, slot, self.me], self.axis, peer
        )
        copy.start()
        self.pending.append(copy)

    def arrived(self, slot, peer, ref):
        remote(
            ref, ref, self.sems.at[0, slot, peer], self.sems.at[1, slot, peer], self.axis, peer
        ).wait_recv()

    def drain(self, count=None):
        count = len(self.pending) if count is None else count
        for copy in self.pending[:count]:
            copy.wait_send()
        self.pending = self.pending[count:]


def build_kernel(
    num_doc, num_feat, subs, scale, prepare,
    docs_ref, dir_ref, phase_hbm, amp_hbm,
    feat_ref, featt_ref, gram_ref,
    dpart, phase_ref, amp_ref, dirs, gsum, gsend, grecv,
    part_sems, row_sems, dir_sems, gram_sems, local_sem, table_sems,
):
    n = docs_ref.shape[1]
    chunk = dirs.shape[2]
    wide = chunk // subs
    me = lax.axis_index("doc")
    fme = lax.axis_index("feat")
    tables = [
        pltpu.make_async_copy(docs_ref, dpart.at[fme, me], table_sems.at[2]),
        pltpu.make_async_copy(phase_hbm.at[me], phase_ref, table_sems.at[0]),
        pltpu.make_async_copy(amp_hbm.at[me], amp_ref, table_sems.at[1]),
    ]
    for table in tables:
        table.start()
    local = pltpu.make_async_copy(
        dir_ref.at[:, pl.ds(pl.multiple_of(me * chunk, chunk), chunk)], dirs.at[me], local_sem
    )
    local.start()
    greet(num_doc, num_feat)
    ch_part = Channel(part_sems, "feat", num_feat)
    ch_row = Channel(row_sems, "doc", num_doc)
    ch_dir = Channel(dir_sems, "doc", num_doc)
    ch_gram = Channel(gram_sems, "doc", num_doc)
    for peer in ch_row.peers():
        ch_row.send(0, peer, docs_ref, dpart.at[fme, me])
    def send_dirs(s):
        for peer in ch_dir.peers():
            cols = pl.ds(pl.multiple_of(peer * chunk + s * wide, wide), wide)
            ch_dir.send(
                s, peer, dir_ref.at[:, cols], dirs.at[me, :, pl.ds(s * wide, wide)]
            )

    for s in range(min(WINDOW, subs)):
        send_dirs(s)
    tables[0].wait()
    for peer in ch_row.peers():
        ch_row.arrived(0, peer, dpart.at[fme, peer])
    for peer in ch_part.peers():
        ch_part.send(0, peer, dpart.at[fme], dpart.at[fme])
    for peer in ch_part.peers():
        ch_part.arrived(0, peer, dpart.at[peer])
    inputs = num_feat * docs_ref.shape[0]
    full = jnp.concatenate([dpart[:, i].reshape(inputs, n).T for i in range(num_doc)], axis=0)
    prepare()
    local.wait()
    for table in tables[1:]:
        table.wait()
    phase = phase_ref[...]
    amp = scale * amp_ref[...]
    for s in range(subs):
        cols = slice(s * wide, (s + 1) * wide)
        for peer in ch_dir.peers():
            ch_dir.arrived(s, peer, dirs.at[peer, :, pl.ds(s * wide, wide)])
        if s + WINDOW < subs:
            ch_dir.drain(num_doc - 1)
            send_dirs(s + WINDOW)
        piece = dirs[:, :, cols].reshape(full.shape[1], wide)
        angles = jnp.dot(full, piece, preferred_element_type=jnp.float32)
        feats = amp[:, cols] * cosine(angles + phase[:, cols])
        high, low = split(feats)
        feat_ref[0, :, cols], feat_ref[1, :, cols] = high, low
        for i in range(num_doc):
            block = slice(i * n, (i + 1) * n)
            both = lax.dot_general(
                high[block],
                jnp.concatenate([high[block], low[block]], axis=0),
                (((1,), (1,)), ((), ())),
                preferred_element_type=jnp.float32,
            )
            rest = lax.dot_general(
                low[block], high[block], (((1,), (1,)), ((), ())), preferred_element_type=jnp.float32
            )
            term = both[:, :n] + (both[:, n:] + rest)
            if s == 0:
                gsum[i] = term
            else:
                gsum[i] += term
        featt_ref[0, cols, :], featt_ref[1, cols, :] = split(feats.T)
    for k in range(1, num_doc + 1):
        peer = lax.rem(me + k, num_doc)
        gsend[peer] = pack_symmetric(gsum[peer])
        if k < num_doc:
            ch_gram.send(0, peer, gsend.at[peer], grecv.at[me])
    total = gsend[me]
    for peer in ch_gram.peers():
        ch_gram.arrived(0, peer, grecv.at[peer])
        total += grecv[peer]
    gram_ref[...] = unpack_symmetric(total)
    for channel in (ch_part, ch_row, ch_dir, ch_gram):
        channel.drain()


def pack_symmetric(values):
    half = values.shape[0] // 2
    rows = lax.broadcasted_iota(jnp.int32, (half, 2 * half), 0)
    lanes = lax.broadcasted_iota(jnp.int32, (half, 2 * half), 1)
    top, bottom = values[:half], values[half:]
    both = jnp.where(lanes <= rows + half, bottom, pltpu.roll(top, half, 1))
    diagonal = jnp.sum(jnp.where(rows == lanes, top, 0.0), axis=0, keepdims=True)
    return jnp.concatenate([both, jnp.broadcast_to(diagonal, (8, 2 * half))], axis=0)


def unpack_symmetric(packed):
    half = packed.shape[0] - 8
    rows = lax.broadcasted_iota(jnp.int32, (half, 2 * half), 0)
    lanes = lax.broadcasted_iota(jnp.int32, (half, 2 * half), 1)
    both, diagonal = packed[:half], packed[half : half + 1]
    flipped = jnp.concatenate([both, both], axis=0).T
    bottom = jnp.where(lanes <= rows + half, both, flipped[half:])
    corner = jnp.where(lanes > rows, pltpu.roll(both, half, 1), flipped[half:])
    corner = jnp.where(lanes == rows, diagonal, corner)
    return jnp.concatenate([jnp.where(lanes >= half, flipped[:half], corner), bottom], axis=0)


def three_left(values):
    high, low = split(values)
    return jnp.concatenate([high, high, low], axis=1)


def three_right(values):
    high, low = split(values)
    return jnp.concatenate([high, low, high], axis=0)


def three_dot(left, right):
    return jnp.dot(left, right, preferred_element_type=jnp.float32)


def invert(gram):
    n = gram.shape[0]
    rows = lax.broadcasted_iota(jnp.int32, (n, n), 0)
    lanes = lax.broadcasted_iota(jnp.int32, (n, n), 1)
    eye = jnp.where(rows == lanes, 1.0, 0.0)
    matrix = gram + eye
    bound = jnp.max(jnp.sum(jnp.abs(matrix), axis=0, keepdims=True), axis=1, keepdims=True)
    first = 2.0 / (1.0 + bound)
    error = (bound - 1.0) / (bound + 1.0)
    near = first * matrix
    guess = first * eye
    for k in range(INVERSE_STEPS):
        scale = 2.0 / (2.0 - error * error)
        error = 0.5 * error * error * scale
        if k == 0:
            moved = jnp.concatenate([first * near, three_dot(three_left(near), three_right(near))], axis=1)
        else:
            moved = three_dot(
                three_left(near), three_right(jnp.concatenate([guess, near], axis=1))
            )
        guess = scale * (2.0 * guess - moved[:, :n])
        near = scale * (2.0 * near - moved[:, n:])
    missing = eye - jnp.dot(matrix, guess, precision=HI)
    return guess + three_dot(three_left(guess), three_right(missing))


def fold(values):
    return jnp.sum(values.reshape(values.shape[0] // 8, 8, values.shape[1]), axis=0)


def admm_kernel(
    num_doc, num_feat, subs,
    feat_ref, featt_ref, inv_ref, signs_ref, weight_ref, start_ref,
    m_ref, w_ref,
    solved, solved_step, part, yrecv, cbuf, psend, psend_step, precv, precv_step,
    norms, z, lastmove, lastlift, wcode, wstep,
    s_sems, y_sems, c_sems, p_sems, norm_sems, w_sems,
):
    n = inv_ref.shape[0]
    chunk = z.shape[0]
    share = n // num_feat
    wide = chunk // subs
    me = lax.axis_index("doc")
    fme = lax.axis_index("feat")
    ch_s = Channel(s_sems, "doc", num_doc)
    ch_y = Channel(y_sems, "feat", num_feat)
    ch_c = Channel(c_sems, "feat", num_feat)
    ch_p = Channel(p_sems, "doc", num_doc)
    own = pl.ds(pl.multiple_of(fme * share, share), share)
    signs = signs_ref[own, :]
    weight = weight_ref[own, :]
    margins = start_ref[own, :]
    duals = jnp.zeros((share, C), jnp.float32)
    rho = jnp.ones((1, 1), jnp.float32)
    inv = inv_ref[...]
    target = start_ref[...] / num_feat
    residue = target
    growth = None

    mine = me * num_feat + fme
    others = [
        (lax.rem(me + i, num_doc), lax.rem(fme + j, num_feat))
        for i in range(num_doc)
        for j in range(num_feat)
        if i or j
    ]

    def norm_copy(step, target):
        row = norms.at[step, mine]
        return pltpu.make_async_remote_copy(
            src_ref=row,
            dst_ref=row,
            send_sem=norm_sems.at[0, step],
            recv_sem=norm_sems.at[1, step],
            device_id={"doc": target[0], "feat": target[1]},
            device_id_type=MESH,
        )

    def norm_all(step):
        rows = norms.at[step, pl.ds(0, len(others))]
        return remote(rows, rows, norm_sems.at[0, step], norm_sems.at[1, step], "doc", others[-1][0])

    groups = wstep.shape[2]
    rows_per = wide // groups

    def w_copy(direction, src, s, peer):
        return [
            remote(
                ref.at[src, s], ref.at[src, s],
                w_sems.at[direction, k, 0, src, s], w_sems.at[direction, k, 1, src, s], "doc", peer,
            )
            for k, ref in enumerate((wcode, wstep))
        ]

    def w_write(src, s):
        for g in range(groups):
            first = pl.multiple_of(src * chunk + s * wide + g * rows_per, rows_per)
            piece = wcode[src, s, g * rows_per : (g + 1) * rows_per, :]
            w_ref[pl.ds(first, rows_per), :] = decode(piece, wstep[src, s, g])

    def send_margins(step):
        for peer in ch_c.peers():
            ch_c.send(step, peer, cbuf.at[step, fme], cbuf.at[step, fme])

    for step in range(ITERS):
        last = step + 1 == ITERS
        if step == 0:
            answer = three_dot(inv, three_right(residue))
        applied = residue - answer
        new_part = target - answer
        solved[step, me], solved_step[step, me] = encode(answer)
        part[step] = new_part
        for peer in ch_s.peers():
            ch_s.send(2 * step, peer, solved.at[step, me], solved.at[step, me])
            ch_s.send(2 * step + 1, peer, solved_step.at[step, me], solved_step.at[step, me])
        for peer in ch_y.peers():
            rows = pl.ds(pl.multiple_of(peer * share, share), share)
            ch_y.send(step, peer, part.at[step, rows, :], yrecv.at[step, fme])
        yrecv[step, fme] = part[step, own, :]
        for peer in ch_y.peers():
            ch_y.arrived(step, peer, yrecv.at[step, peer])
        sums = yrecv[step, 0]
        for k in range(1, num_feat):
            sums += yrecv[step, k]
        old_margins = margins
        margins = logistic_prox(sums + duals, signs, weight / rho)
        duals = duals + sums - margins
        cbuf[step, fme, 0] = margins if last else (margins - sums) / num_feat
        cbuf[step, fme, 1] = duals / num_feat
        send_margins(step)
        for peer in ch_s.peers():
            ch_s.arrived(2 * step, peer, solved.at[step, peer])
            ch_s.arrived(2 * step + 1, peer, solved_step.at[step, peer])
        everything = jnp.concatenate(
            split(decode(solved[step], solved_step[step]).reshape(num_doc * n, C)), axis=1
        )
        limit = shrink_level / (rho * num_doc)
        if not last:
            gap = fold((sums - margins) ** 2) if share > 8 else (sums - margins) ** 2
            shift = (
                fold((margins - old_margins) ** 2) if share > 8 else (margins - old_margins) ** 2
            )
            if step == 0:
                d_answer, d_applied = answer, applied
            else:
                d_answer = answer - last_answer / growth
                d_applied = applied - last_applied / growth
            primal = gap + fold(d_answer * d_applied)
            dual = shift
        for s in range(subs):
            rows = slice(s * wide, (s + 1) * wide)
            lift = split_dot(featt_ref[0, rows, :], featt_ref[1, rows, :], everything)
            if step == 0:
                fresh = shrink_values(lift / num_doc, limit)
                move = -fresh
                d_move, d_lift = move, lift
            else:
                old = z[rows, :]
                fresh = shrink_values(old + lift / num_doc, limit)
                if not last:
                    move = old - fresh
                    d_move = move - lastmove[rows, :] / growth
                    d_lift = lift - lastlift[rows, :] / growth
            if last:
                for g in range(groups):
                    piece = slice(g * rows_per, (g + 1) * rows_per)
                    wcode[me, s, piece, :], wstep[me, s, g] = encode(num_feat * fresh[piece])

                @pl.when(me + 1 < num_doc)
                def _(s=s):
                    for copy in w_copy(0, me, s, me + 1):
                        copy.start()

                @pl.when(me >= 1)
                def _(s=s):
                    for copy in w_copy(1, me, s, me - 1):
                        copy.start()

                w_write(me, s)
            else:
                z[rows, :] = fresh
                lastmove[rows, :] = move
                lastlift[rows, :] = lift
                primal += fold(num_doc * d_move * d_move + 2.0 * d_move * d_lift)
                dual += num_doc * fold(move * move)
        if last:
            break
        norms[step, mine, 0:1] = jnp.sum(primal, axis=0, keepdims=True)
        norms[step, mine, 1:2] = jnp.sum(dual, axis=0, keepdims=True)
        for target in others:
            norm_copy(step, target).start()
        weights = jnp.concatenate(split(z[...]), axis=1)
        for k in range(1, num_doc + 1):
            peer = lax.rem(me + k, num_doc)
            block = pl.ds(pl.multiple_of(peer * n, n), n)
            product = split_dot(feat_ref[0, block, :], feat_ref[1, block, :], weights)
            if k < num_doc:
                psend[step, k - 1], psend_step[step, k - 1] = encode(product)
                ch_p.send(2 * step, peer, psend.at[step, k - 1], precv.at[step, me])
                ch_p.send(2 * step + 1, peer, psend_step.at[step, k - 1], precv_step.at[step, me])
        last_answer, last_applied = answer, applied
        for peer in ch_c.peers():
            ch_c.arrived(step, peer, cbuf.at[step, peer])
        margins_part = cbuf[step, :, 0].reshape(n, C)
        duals_part = cbuf[step, :, 1].reshape(n, C)
        for peer in ch_p.peers():
            ch_p.arrived(2 * step, peer, precv.at[step, peer])
            ch_p.arrived(2 * step + 1, peer, precv_step.at[step, peer])
            product += decode(precv[step, peer], precv_step[step, peer])
        kept = new_part + margins_part - product
        shrunk = applied - product - duals_part if step == 0 else (
            old_product - product + applied - duals_part
        )
        old_product = product
        both = three_dot(inv, three_right(jnp.concatenate([kept, shrunk], axis=1)))
        norm_all(step).wait_recv()
        sums_of = jnp.sum(jnp.sum(norms[step], axis=0), axis=1, keepdims=True)
        primal = jnp.maximum(sums_of[0:1], 0.0)
        dual = sums_of[1:2]
        growth = jnp.sqrt(
            jnp.sqrt((primal + ratio_floor) / (rho * rho * dual + ratio_floor))
        )
        rho = rho * growth
        shrink = 1.0 / growth
        duals = duals * shrink
        target = new_part + margins_part - duals_part * shrink
        residue = kept + shrunk * shrink
        answer = both[:, :C] + both[:, C:] * shrink
    for hop in range(1, num_doc):
        for s in range(subs):

            @pl.when(me >= hop)
            def _(hop=hop, s=s):
                for copy in w_copy(0, me - hop, s, me):
                    copy.wait_recv()

                @pl.when(me + 1 < num_doc)
                def _():
                    for copy in w_copy(0, me - hop, s, me + 1):
                        copy.start()

                w_write(me - hop, s)

            @pl.when(me + hop < num_doc)
            def _(hop=hop, s=s):
                for copy in w_copy(1, me + hop, s, me):
                    copy.wait_recv()

                @pl.when(me >= 1)
                def _():
                    for copy in w_copy(1, me + hop, s, me - 1):
                        copy.start()

                w_write(me + hop, s)

    for peer in ch_c.peers():
        ch_c.arrived(ITERS - 1, peer, cbuf.at[ITERS - 1, peer])
    m_ref[...] = cbuf[ITERS - 1, :, 0].reshape(n, C)
    for hop in range(num_doc):
        for s in range(subs):

            @pl.when((me >= hop) & (me + 1 < num_doc))
            def _(hop=hop, s=s):
                for copy in w_copy(0, me - hop, s, me + 1):
                    copy.wait_send()

            @pl.when((me + hop < num_doc) & (me >= 1))
            def _(hop=hop, s=s):
                for copy in w_copy(1, me + hop, s, me - 1):
                    copy.wait_send()

    for channel in (ch_s, ch_y, ch_c, ch_p):
        channel.drain()
    for step in range(ITERS - 1):
        norm_all(step).wait_send()


def whole_kernel(
    num_doc, num_feat, subs, dir_subs, scale,
    docs_ref, dir_ref, phase_hbm, amp_hbm, lab_hbm, dw_hbm,
    m_ref, w_ref,
    feat_ref, featt_ref, gram_ref, inv_ref,
    lab_ref, dw_ref, signs_ref, weight_ref, start_ref, small_sems,
    *scratch,
):
    n = gram_ref.shape[0]
    smalls = [
        pltpu.make_async_copy(lab_hbm, lab_ref, small_sems.at[0]),
        pltpu.make_async_copy(dw_hbm, dw_ref, small_sems.at[1]),
    ]
    for small in smalls:
        small.start()

    def prepare():
        for small in smalls:
            small.wait()
        classes = lax.broadcasted_iota(jnp.int32, (n, C), 1).astype(jnp.float32)
        spread = jnp.broadcast_to(lab_ref[...].astype(jnp.float32), (C, n)).T
        weight = jnp.broadcast_to(dw_ref[...], (C, n)).T
        signs = jnp.where(spread == classes, 1.0, -1.0)
        signs_ref[...] = signs
        weight_ref[...] = weight
        start_ref[...] = logistic_prox(jnp.zeros((n, C), jnp.float32), signs, weight)

    build_kernel(
        num_doc, num_feat, dir_subs, scale, prepare,
        docs_ref, dir_ref, phase_hbm, amp_hbm, feat_ref, featt_ref, gram_ref, *scratch[:13],
    )
    inv_ref[...] = three_left(invert(gram_ref[...]))
    admm_kernel(
        num_doc, num_feat, subs,
        feat_ref, featt_ref, inv_ref, signs_ref, weight_ref, start_ref, m_ref, w_ref,
        *scratch[13:],
    )


def hand_over(margins_ref, weights_ref, m_ref, w_ref, sems):
    copies = [
        pltpu.make_async_copy(margins_ref, m_ref, sems.at[0]),
        pltpu.make_async_copy(weights_ref, w_ref, sems.at[1]),
    ]
    for copy in copies:
        copy.start()
    for copy in copies:
        copy.wait()


def per_device(documents, directions, phase, amplitude, doc_weight, labels):
    n, local_inputs = documents.shape
    input_rows, width_tile = directions.shape
    num_feat = lax.axis_size("feat")
    num_doc = lax.axis_size("doc")
    chunk = width_tile // num_doc
    subs = max(1, min(4, chunk // 128))
    dir_subs = max(1, min(DIR_SUBS, chunk // 128))
    share = n // num_feat
    f32, bf16 = jnp.float32, jnp.bfloat16
    vmem = pl.BlockSpec(memory_space=pltpu.VMEM)
    dma = pltpu.SemaphoreType.DMA
    shape = jax.ShapeDtypeStruct
    rounds = ITERS - 1
    anywhere = pl.BlockSpec(memory_space=pl.ANY)
    groups = max(1, chunk // subs // n)
    operands = (
        documents.T,
        directions,
        phase.reshape(num_doc, 1, chunk),
        amplitude.reshape(num_doc, 1, chunk),
        labels.reshape(1, n),
        doc_weight.reshape(1, n),
    )
    margins, weights = pl.pallas_call(
        functools.partial(
            whole_kernel, num_doc, num_feat, subs, dir_subs, (2.0 / width_tile) ** 0.5
        ),
        out_shape=(shape((n, C), f32), shape((width_tile, C), f32)),
        in_specs=[anywhere] * 6,
        out_specs=(vmem, vmem),
        scratch_shapes=[
            pltpu.VMEM((2, num_doc * n, chunk), bf16),
            pltpu.VMEM((2, chunk, num_doc * n), bf16),
            pltpu.VMEM((n, n), f32),
            pltpu.VMEM((n, 3 * n), bf16),
            pltpu.VMEM((1, n), jnp.int32),
            pltpu.VMEM((1, n), f32),
            pltpu.VMEM((n, C), f32),
            pltpu.VMEM((n, C), f32),
            pltpu.VMEM((n, C), f32),
            dma((2,)),
            pltpu.VMEM((num_feat, num_doc, local_inputs, n), bf16),
            pltpu.VMEM((1, chunk), f32),
            pltpu.VMEM((1, chunk), f32),
            pltpu.VMEM((num_doc, input_rows, chunk), bf16),
            pltpu.VMEM((num_doc, n, n), f32),
            pltpu.VMEM((num_doc, n // 2 + 8, n), f32),
            pltpu.VMEM((num_doc, n // 2 + 8, n), f32),
            dma((2, 1, num_feat)),
            dma((2, 1, num_doc)),
            dma((2, dir_subs, num_doc)),
            dma((2, 1, num_doc)),
            dma,
            dma((3,)),
            pltpu.VMEM((ITERS, num_doc, n, C), jnp.int16),
            pltpu.VMEM((ITERS, num_doc, 1, C), f32),
            pltpu.VMEM((ITERS, n, C), f32),
            pltpu.VMEM((ITERS, num_feat, share, C), f32),
            pltpu.VMEM((ITERS, num_feat, 2, share, C), f32),
            pltpu.VMEM((rounds, num_doc, n, C), jnp.int16),
            pltpu.VMEM((rounds, num_doc, 1, C), f32),
            pltpu.VMEM((rounds, num_doc, n, C), jnp.int16),
            pltpu.VMEM((rounds, num_doc, 1, C), f32),
            pltpu.VMEM((rounds, num_doc * num_feat, 2, C), f32),
            pltpu.VMEM((chunk, C), f32),
            pltpu.VMEM((chunk, C), f32),
            pltpu.VMEM((chunk, C), f32),
            pltpu.VMEM((num_doc, subs, chunk // subs, C), jnp.int16),
            pltpu.VMEM((num_doc, subs, groups, 1, C), f32),
            dma((2, 2 * ITERS, num_doc)),
            dma((2, ITERS, num_feat)),
            dma((2, ITERS, num_feat)),
            dma((2, 2 * rounds, num_doc)),
            dma((2, rounds)),
            dma((2, 2, 2, num_doc, subs)),
        ],
        compiler_params=pltpu.CompilerParams(
            collective_id=0, has_side_effects=True, vmem_limit_bytes=48 * 1024 * 1024
        ),
        name="admm",
    )(*[pltpu.with_memory_space_constraint(operand, pltpu.HBM) for operand in operands])
    return pl.pallas_call(
        hand_over,
        out_shape=(shape((n, C), f32), shape((width_tile, C), f32)),
        in_specs=[anywhere] * 2,
        out_specs=(anywhere,) * 2,
        scratch_shapes=[dma((2,))],
        compiler_params=pltpu.CompilerParams(vmem_limit_bytes=1024 * 1024),
        name="hand_over",
    )(margins, weights)


def solution(mesh):
    in_specs = (P("doc", "feat"), P("doc", "feat"), P("feat"), P("feat"), P("doc"), P("doc"))
    out_specs = (P("doc", None), P("feat", None))
    return jax.shard_map(
        per_device, mesh=mesh, in_specs=in_specs, out_specs=out_specs, check_vma=False
    )
```

```python
import functools

import jax
import jax.numpy as jnp
from jax import lax
from jax.experimental import pallas as pl
from jax.experimental.pallas import tpu as pltpu
from jax.sharding import PartitionSpec as P

C = 128
ITERS = 3
NEWTON = 3
LEVELS = 32767.0
INVERSE_STEPS = 7
DIR_SUBS = 2
HI = lax.Precision.HIGHEST
MESH = pl.DeviceIdType.MESH

shrink_level = 0.1
ratio_floor = 1e-06


def logistic_prox(target, signs, weight_ratio):
    current = target
    for newton_step in range(NEWTON):
        chance = 1.0 / (1.0 + jnp.exp(signs * current))
        gradient = current - target - weight_ratio * signs * chance
        current = current - gradient / (1.0 + weight_ratio * chance * (1.0 - chance))
    return current


def shrink_values(target, limit):
    return target - jnp.minimum(jnp.maximum(target, -limit), limit)


def cosine(angle):
    turns = jnp.floor(angle * 0.3183098861837907 + 0.5)
    rest = angle - turns * 3.140625
    rest = rest - turns * 9.67502593994140625e-4
    rest = rest - turns * 1.509957990978376432e-7
    odd = turns - 2.0 * jnp.floor(turns * 0.5)
    sq = rest * rest
    poly = 2.08767569878681e-9
    poly = poly * sq - 2.755731922398589e-7
    poly = poly * sq + 2.48015873015873e-5
    poly = poly * sq - 1.388888888888889e-3
    poly = poly * sq + 4.1666666666666664e-2
    poly = poly * sq - 0.5
    poly = poly * sq + 1.0
    return poly * (1.0 - 2.0 * odd)


def split(values):
    high = values.astype(jnp.bfloat16)
    return high, (values - high.astype(jnp.float32)).astype(jnp.bfloat16)


def split_dot(high, low, pair):
    both = jnp.dot(high, pair, preferred_element_type=jnp.float32)
    rest = jnp.dot(low, pair[:, :C], preferred_element_type=jnp.float32)
    return both[:, :C] + (both[:, C:] + rest)


def encode(values):
    largest = jnp.max(jnp.abs(values), axis=0, keepdims=True)
    steps = jnp.where(largest > 0.0, LEVELS / largest, 0.0)
    codes = jnp.floor(values * steps + 0.5).astype(jnp.int32).astype(jnp.int16)
    return codes, largest * (1.0 / LEVELS)


def decode(codes, steps):
    return codes.astype(jnp.int32).astype(jnp.float32) * steps


def remote(src, dst, send_sem, recv_sem, axis, peer):
    return pltpu.make_async_remote_copy(
        src_ref=src,
        dst_ref=dst,
        send_sem=send_sem,
        recv_sem=recv_sem,
        device_id={axis: peer},
        device_id_type=MESH,
    )


def greet(num_doc, num_feat):
    barrier = pltpu.get_barrier_semaphore()
    for axis, size in (("doc", num_doc), ("feat", num_feat)):
        me = lax.axis_index(axis)
        for k in range(1, size):
            pl.semaphore_signal(
                barrier, inc=1, device_id={axis: lax.rem(me + k, size)}, device_id_type=MESH
            )
    pl.semaphore_wait(barrier, num_doc + num_feat - 2)


class Gather:
    def __init__(self, sems, axis, size):
        self.sems, self.axis, self.size = sems, axis, size
        self.me = lax.axis_index(axis)

    def peers(self):
        return [lax.rem(self.me + k, self.size) for k in range(1, self.size)]

    def send(self, step, peer, src, dst):
        remote(src, dst, self.sems.at[0, step], self.sems.at[1, step], self.axis, peer).start()

    def all_of(self, step, rows):
        return remote(
            rows, rows, self.sems.at[0, step], self.sems.at[1, step], self.axis, self.peers()[0]
        )

    def rows(self, ref, *where):
        return ref.at[(*where, pl.ds(0, self.size - 1))]


def build_kernel(
    num_doc, num_feat, subs, scale, prepare,
    docs_ref, dir_ref, phase_hbm, amp_hbm,
    feat_ref, featt_ref, gram_ref,
    dpart, phase_ref, amp_ref, dirs, gsum, gsend, grecv,
    part_sems, row_sems, dir_sems, gram_sems, local_sem, table_sems,
):
    n = docs_ref.shape[1]
    chunk = dirs.shape[2]
    wide = chunk // subs
    me = lax.axis_index("doc")
    fme = lax.axis_index("feat")
    tables = [
        pltpu.make_async_copy(docs_ref, dpart.at[fme, me], table_sems.at[2]),
        pltpu.make_async_copy(phase_hbm.at[me], phase_ref, table_sems.at[0]),
        pltpu.make_async_copy(amp_hbm.at[me], amp_ref, table_sems.at[1]),
    ]
    for table in tables:
        table.start()
    local = pltpu.make_async_copy(
        dir_ref.at[:, pl.ds(pl.multiple_of(me * chunk, chunk), chunk)], dirs.at[me], local_sem
    )
    local.start()
    greet(num_doc, num_feat)
    ch_part = Gather(part_sems, "feat", num_feat)
    ch_row = Gather(row_sems, "doc", num_doc)
    ch_dir = Gather(dir_sems, "doc", num_doc)
    ch_gram = Gather(gram_sems, "doc", num_doc)
    for peer in ch_row.peers():
        ch_row.send(0, peer, docs_ref, dpart.at[fme, me])
    def send_dirs(s):
        for peer in ch_dir.peers():
            cols = pl.ds(pl.multiple_of(peer * chunk + s * wide, wide), wide)
            ch_dir.send(
                s, peer, dir_ref.at[:, cols], dirs.at[me, :, pl.ds(s * wide, wide)]
            )

    def dir_rows(s):
        return dirs.at[pl.ds(0, num_doc - 1), :, pl.ds(s * wide, wide)]

    for s in range(subs):
        send_dirs(s)
    tables[0].wait()
    ch_row.all_of(0, ch_row.rows(dpart, fme)).wait_recv()
    for peer in ch_part.peers():
        ch_part.send(0, peer, dpart.at[fme], dpart.at[fme])
    ch_part.all_of(0, ch_part.rows(dpart)).wait_recv()
    inputs = num_feat * docs_ref.shape[0]
    full = jnp.concatenate([dpart[:, i].reshape(inputs, n).T for i in range(num_doc)], axis=0)
    prepare()
    local.wait()
    for table in tables[1:]:
        table.wait()
    phase = phase_ref[...]
    amp = scale * amp_ref[...]
    for s in range(subs):
        cols = slice(s * wide, (s + 1) * wide)
        ch_dir.all_of(s, dir_rows(s)).wait_recv()
        piece = dirs[:, :, cols].reshape(full.shape[1], wide)
        angles = jnp.dot(full, piece, preferred_element_type=jnp.float32)
        feats = amp[:, cols] * cosine(angles + phase[:, cols])
        high, low = split(feats)
        feat_ref[0, :, cols], feat_ref[1, :, cols] = high, low
        for i in range(num_doc):
            block = slice(i * n, (i + 1) * n)
            both = lax.dot_general(
                high[block],
                jnp.concatenate([high[block], low[block]], axis=0),
                (((1,), (1,)), ((), ())),
                preferred_element_type=jnp.float32,
            )
            rest = lax.dot_general(
                low[block], high[block], (((1,), (1,)), ((), ())), preferred_element_type=jnp.float32
            )
            term = both[:, :n] + (both[:, n:] + rest)
            if s == 0:
                gsum[i] = term
            else:
                gsum[i] += term
        featt_ref[0, cols, :], featt_ref[1, cols, :] = split(feats.T)
    for k in range(1, num_doc + 1):
        peer = lax.rem(me + k, num_doc)
        gsend[peer] = pack_symmetric(gsum[peer])
        if k < num_doc:
            ch_gram.send(0, peer, gsend.at[peer], grecv.at[me])
    total = gsend[me]
    ch_gram.all_of(0, ch_gram.rows(grecv)).wait_recv()
    for peer in ch_gram.peers():
        total += grecv[peer]
    gram_ref[...] = unpack_symmetric(total)
    return [
        ch_row.all_of(0, ch_row.rows(dpart, fme)),
        ch_part.all_of(0, ch_part.rows(dpart)),
        ch_gram.all_of(0, ch_gram.rows(grecv)),
        *(ch_dir.all_of(s, dir_rows(s)) for s in range(subs)),
    ]


def pack_symmetric(values):
    half = values.shape[0] // 2
    rows = lax.broadcasted_iota(jnp.int32, (half, 2 * half), 0)
    lanes = lax.broadcasted_iota(jnp.int32, (half, 2 * half), 1)
    top, bottom = values[:half], values[half:]
    both = jnp.where(lanes <= rows + half, bottom, pltpu.roll(top, half, 1))
    diagonal = jnp.sum(jnp.where(rows == lanes, top, 0.0), axis=0, keepdims=True)
    return jnp.concatenate([both, jnp.broadcast_to(diagonal, (8, 2 * half))], axis=0)


def unpack_symmetric(packed):
    half = packed.shape[0] - 8
    rows = lax.broadcasted_iota(jnp.int32, (half, 2 * half), 0)
    lanes = lax.broadcasted_iota(jnp.int32, (half, 2 * half), 1)
    both, diagonal = packed[:half], packed[half : half + 1]
    flipped = jnp.concatenate([both, both], axis=0).T
    bottom = jnp.where(lanes <= rows + half, both, flipped[half:])
    corner = jnp.where(lanes > rows, pltpu.roll(both, half, 1), flipped[half:])
    corner = jnp.where(lanes == rows, diagonal, corner)
    return jnp.concatenate([jnp.where(lanes >= half, flipped[:half], corner), bottom], axis=0)


def three_left(values):
    high, low = split(values)
    return jnp.concatenate([high, high, low], axis=1)


def three_right(values):
    high, low = split(values)
    return jnp.concatenate([high, low, high], axis=0)


def three_dot(left, right):
    return jnp.dot(left, right, preferred_element_type=jnp.float32)


def invert(gram):
    n = gram.shape[0]
    rows = lax.broadcasted_iota(jnp.int32, (n, n), 0)
    lanes = lax.broadcasted_iota(jnp.int32, (n, n), 1)
    eye = jnp.where(rows == lanes, 1.0, 0.0)
    matrix = gram + eye
    bound = jnp.max(jnp.sum(jnp.abs(matrix), axis=0, keepdims=True), axis=1, keepdims=True)
    first = 2.0 / (1.0 + bound)
    error = (bound - 1.0) / (bound + 1.0)
    near = first * matrix
    guess = first * eye
    for k in range(INVERSE_STEPS):
        scale = 2.0 / (2.0 - error * error)
        error = 0.5 * error * error * scale
        if k == 0:
            moved = jnp.concatenate([first * near, three_dot(three_left(near), three_right(near))], axis=1)
        else:
            moved = three_dot(
                three_left(near), three_right(jnp.concatenate([guess, near], axis=1))
            )
        guess = scale * (2.0 * guess - moved[:, :n])
        near = scale * (2.0 * near - moved[:, n:])
    missing = eye - jnp.dot(matrix, guess, precision=HI)
    return guess + three_dot(three_left(guess), three_right(missing))


def fold(values):
    return jnp.sum(values.reshape(values.shape[0] // 8, 8, values.shape[1]), axis=0)


def admm_kernel(
    num_doc, num_feat, subs, begun,
    feat_ref, featt_ref, inv_ref, signs_ref, weight_ref, start_ref,
    m_ref, w_ref,
    solved, solved_step, part, yrecv, cbuf, psend, psend_step, precv, precv_step,
    norms, z, lastmove, lastlift, wcode, wstep,
    s_sems, y_sems, c_sems, p_sems, norm_sems, wsend_sems, w_sems,
):
    n = inv_ref.shape[0]
    chunk = z.shape[0]
    share = n // num_feat
    wide = chunk // subs
    me = lax.axis_index("doc")
    fme = lax.axis_index("feat")
    ch_s = Gather(s_sems, "doc", num_doc)
    ch_y = Gather(y_sems, "feat", num_feat)
    ch_c = Gather(c_sems, "feat", num_feat)
    ch_p = Gather(p_sems, "doc", num_doc)
    own = pl.ds(pl.multiple_of(fme * share, share), share)
    signs = signs_ref[own, :]
    weight = weight_ref[own, :]
    margins = start_ref[own, :]
    duals = jnp.zeros((share, C), jnp.float32)
    rho = jnp.ones((1, 1), jnp.float32)
    inv = inv_ref[...]
    target = start_ref[...] / num_feat
    residue = target
    growth = None

    mine = me * num_feat + fme
    others = [
        (lax.rem(me + i, num_doc), lax.rem(fme + j, num_feat))
        for i in range(num_doc)
        for j in range(num_feat)
        if i or j
    ]

    def norm_copy(step, target):
        row = norms.at[step, mine]
        return pltpu.make_async_remote_copy(
            src_ref=row,
            dst_ref=row,
            send_sem=norm_sems.at[0, step],
            recv_sem=norm_sems.at[1, step],
            device_id={"doc": target[0], "feat": target[1]},
            device_id_type=MESH,
        )

    def norm_all(step):
        rows = norms.at[step, pl.ds(0, len(others))]
        return remote(rows, rows, norm_sems.at[0, step], norm_sems.at[1, step], "doc", others[-1][0])

    groups = wstep.shape[2]
    rows_per = wide // groups

    def w_copy(direction, src, s, peer):
        return [
            remote(
                ref.at[src, s], ref.at[src, s],
                wsend_sems.at[direction, k], w_sems.at[k, src, s], "doc", peer,
            )
            for k, ref in enumerate((wcode, wstep))
        ]

    def w_write(src, s):
        for g in range(groups):
            first = pl.multiple_of(src * chunk + s * wide + g * rows_per, rows_per)
            piece = wcode[src, s, g * rows_per : (g + 1) * rows_per, :]
            w_ref[pl.ds(first, rows_per), :] = decode(piece, wstep[src, s, g])

    def s_all(step):
        return [
            ch_s.all_of(2 * step + k, ch_s.rows(ref, step))
            for k, ref in enumerate((solved, solved_step))
        ]

    def p_all(step):
        return [
            ch_p.all_of(2 * step + k, ch_p.rows(ref, step))
            for k, ref in enumerate((precv, precv_step))
        ]

    def send_margins(step):
        for peer in ch_c.peers():
            ch_c.send(step, peer, cbuf.at[step, fme], cbuf.at[step, fme])

    for step in range(ITERS):
        last = step + 1 == ITERS
        if step == 0:
            answer = three_dot(inv, three_right(residue))
        applied = residue - answer
        new_part = target - answer
        solved[step, me], solved_step[step, me] = encode(answer)
        part[step] = new_part
        for peer in ch_s.peers():
            ch_s.send(2 * step, peer, solved.at[step, me], solved.at[step, me])
            ch_s.send(2 * step + 1, peer, solved_step.at[step, me], solved_step.at[step, me])
        for peer in ch_y.peers():
            rows = pl.ds(pl.multiple_of(peer * share, share), share)
            ch_y.send(step, peer, part.at[step, rows, :], yrecv.at[step, fme])
        yrecv[step, fme] = part[step, own, :]
        ch_y.all_of(step, ch_y.rows(yrecv, step)).wait_recv()
        sums = yrecv[step, 0]
        for k in range(1, num_feat):
            sums += yrecv[step, k]
        old_margins = margins
        margins = logistic_prox(sums + duals, signs, weight / rho)
        duals = duals + sums - margins
        cbuf[step, fme, 0] = margins if last else (margins - sums) / num_feat
        cbuf[step, fme, 1] = duals / num_feat
        send_margins(step)
        for copy in s_all(step):
            copy.wait_recv()
        everything = jnp.concatenate(
            split(decode(solved[step], solved_step[step]).reshape(num_doc * n, C)), axis=1
        )
        limit = shrink_level / (rho * num_doc)
        if not last:
            gap = fold((sums - margins) ** 2) if share > 8 else (sums - margins) ** 2
            shift = (
                fold((margins - old_margins) ** 2) if share > 8 else (margins - old_margins) ** 2
            )
            if step == 0:
                d_answer, d_applied = answer, applied
            else:
                d_answer = answer - last_answer / growth
                d_applied = applied - last_applied / growth
            primal = gap + fold(d_answer * d_applied)
            dual = shift
        for s in range(subs):
            rows = slice(s * wide, (s + 1) * wide)
            lift = split_dot(featt_ref[0, rows, :], featt_ref[1, rows, :], everything)
            if step == 0:
                fresh = shrink_values(lift / num_doc, limit)
                move = -fresh
                d_move, d_lift = move, lift
            else:
                old = z[rows, :]
                fresh = shrink_values(old + lift / num_doc, limit)
                if not last:
                    move = old - fresh
                    d_move = move - lastmove[rows, :] / growth
                    d_lift = lift - lastlift[rows, :] / growth
            if last:
                for g in range(groups):
                    piece = slice(g * rows_per, (g + 1) * rows_per)
                    wcode[me, s, piece, :], wstep[me, s, g] = encode(num_feat * fresh[piece])

                @pl.when(me + 1 < num_doc)
                def _(s=s):
                    for copy in w_copy(0, me, s, me + 1):
                        copy.start()

                @pl.when(me >= 1)
                def _(s=s):
                    for copy in w_copy(1, me, s, me - 1):
                        copy.start()

                w_write(me, s)
            else:
                z[rows, :] = fresh
                lastmove[rows, :] = move
                lastlift[rows, :] = lift
                primal += fold(num_doc * d_move * d_move + 2.0 * d_move * d_lift)
                dual += num_doc * fold(move * move)
        if last:
            break
        norms[step, mine, 0:1] = jnp.sum(primal, axis=0, keepdims=True)
        norms[step, mine, 1:2] = jnp.sum(dual, axis=0, keepdims=True)
        for target in others:
            norm_copy(step, target).start()
        weights = jnp.concatenate(split(z[...]), axis=1)
        for k in range(1, num_doc + 1):
            peer = lax.rem(me + k, num_doc)
            block = pl.ds(pl.multiple_of(peer * n, n), n)
            product = split_dot(feat_ref[0, block, :], feat_ref[1, block, :], weights)
            if k < num_doc:
                psend[step, k - 1], psend_step[step, k - 1] = encode(product)
                ch_p.send(2 * step, peer, psend.at[step, k - 1], precv.at[step, me])
                ch_p.send(2 * step + 1, peer, psend_step.at[step, k - 1], precv_step.at[step, me])
        last_answer, last_applied = answer, applied
        ch_c.all_of(step, ch_c.rows(cbuf, step)).wait_recv()
        margins_part = cbuf[step, :, 0].reshape(n, C)
        duals_part = cbuf[step, :, 1].reshape(n, C)
        for copy in p_all(step):
            copy.wait_recv()
        for peer in ch_p.peers():
            product += decode(precv[step, peer], precv_step[step, peer])
        kept = new_part + margins_part - product
        shrunk = applied - product - duals_part if step == 0 else (
            old_product - product + applied - duals_part
        )
        old_product = product
        both = three_dot(inv, three_right(jnp.concatenate([kept, shrunk], axis=1)))
        norm_all(step).wait_recv()
        sums_of = jnp.sum(jnp.sum(norms[step], axis=0), axis=1, keepdims=True)
        primal = jnp.maximum(sums_of[0:1], 0.0)
        dual = sums_of[1:2]
        growth = jnp.sqrt(
            jnp.sqrt((primal + ratio_floor) / (rho * rho * dual + ratio_floor))
        )
        rho = rho * growth
        shrink = 1.0 / growth
        duals = duals * shrink
        target = new_part + margins_part - duals_part * shrink
        residue = kept + shrunk * shrink
        answer = both[:, :C] + both[:, C:] * shrink
    def w_sent(direction, count):
        for k, ref in enumerate((wcode, wstep)):
            rows = ref.at[pl.ds(0, count)]
            remote(
                rows, rows, wsend_sems.at[direction, k], w_sems.at[k, 0, 0], "doc", lax.rem(me + 1, num_doc)
            ).wait_send()

    for step in range(ITERS):
        begun += s_all(step)
        if step + 1 < ITERS:
            begun += [*p_all(step), norm_all(step)]
    for copy in begun:
        copy.wait_send()
    for hop in range(1, num_doc):
        if hop == min(2, num_doc - 1):
            ch_c.all_of(ITERS - 1, ch_c.rows(cbuf, ITERS - 1)).wait_recv()
            m_ref[...] = cbuf[ITERS - 1, :, 0].reshape(n, C)
            for step in range(ITERS):
                ch_y.all_of(step, ch_y.rows(yrecv, step)).wait_send()
                ch_c.all_of(step, ch_c.rows(cbuf, step)).wait_send()
        for s in range(subs):

            @pl.when(me >= hop)
            def _(hop=hop, s=s):
                for copy in w_copy(0, me - hop, s, me):
                    copy.wait_recv()

                @pl.when(me + 1 < num_doc)
                def _():
                    for copy in w_copy(0, me - hop, s, me + 1):
                        copy.start()

                w_write(me - hop, s)

            @pl.when(me + hop < num_doc)
            def _(hop=hop, s=s):
                for copy in w_copy(1, me + hop, s, me):
                    copy.wait_recv()

                @pl.when(me >= 1)
                def _():
                    for copy in w_copy(1, me + hop, s, me - 1):
                        copy.start()

                w_write(me + hop, s)

    for count in range(1, num_doc):

        @pl.when(me + 1 == count)
        def _(count=count):
            w_sent(0, count)

        @pl.when(me + count == num_doc)
        def _(count=count):
            w_sent(1, count)


def whole_kernel(
    num_doc, num_feat, subs, dir_subs, scale,
    docs_ref, dir_ref, phase_hbm, amp_hbm, lab_hbm, dw_hbm,
    m_ref, w_ref,
    feat_ref, featt_ref, gram_ref, inv_ref,
    lab_ref, dw_ref, signs_ref, weight_ref, start_ref, small_sems,
    *scratch,
):
    n = gram_ref.shape[0]
    smalls = [
        pltpu.make_async_copy(lab_hbm, lab_ref, small_sems.at[0]),
        pltpu.make_async_copy(dw_hbm, dw_ref, small_sems.at[1]),
    ]
    for small in smalls:
        small.start()

    def prepare():
        for small in smalls:
            small.wait()
        classes = lax.broadcasted_iota(jnp.int32, (n, C), 1).astype(jnp.float32)
        spread = jnp.broadcast_to(lab_ref[...].astype(jnp.float32), (C, n)).T
        weight = jnp.broadcast_to(dw_ref[...], (C, n)).T
        signs = jnp.where(spread == classes, 1.0, -1.0)
        signs_ref[...] = signs
        weight_ref[...] = weight
        start_ref[...] = logistic_prox(jnp.zeros((n, C), jnp.float32), signs, weight)

    begun = build_kernel(
        num_doc, num_feat, dir_subs, scale, prepare,
        docs_ref, dir_ref, phase_hbm, amp_hbm, feat_ref, featt_ref, gram_ref, *scratch[:13],
    )
    inv_ref[...] = three_left(invert(gram_ref[...]))
    admm_kernel(
        num_doc, num_feat, subs, begun,
        feat_ref, featt_ref, inv_ref, signs_ref, weight_ref, start_ref, m_ref, w_ref,
        *scratch[13:],
    )


def hand_over(margins_ref, weights_ref, m_ref, w_ref, sems):
    copies = [
        pltpu.make_async_copy(margins_ref, m_ref, sems.at[0]),
        pltpu.make_async_copy(weights_ref, w_ref, sems.at[1]),
    ]
    for copy in copies:
        copy.start()
    for copy in copies:
        copy.wait()


def per_device(documents, directions, phase, amplitude, doc_weight, labels):
    n, local_inputs = documents.shape
    input_rows, width_tile = directions.shape
    num_feat = lax.axis_size("feat")
    num_doc = lax.axis_size("doc")
    chunk = width_tile // num_doc
    subs = max(1, min(4, chunk // 128))
    dir_subs = max(1, min(DIR_SUBS, chunk // 128))
    share = n // num_feat
    f32, bf16 = jnp.float32, jnp.bfloat16
    vmem = pl.BlockSpec(memory_space=pltpu.VMEM)
    dma = pltpu.SemaphoreType.DMA
    shape = jax.ShapeDtypeStruct
    rounds = ITERS - 1
    anywhere = pl.BlockSpec(memory_space=pl.ANY)
    groups = max(1, chunk // subs // n)
    operands = (
        documents.T,
        directions,
        phase.reshape(num_doc, 1, chunk),
        amplitude.reshape(num_doc, 1, chunk),
        labels.reshape(1, n),
        doc_weight.reshape(1, n),
    )
    margins, weights = pl.pallas_call(
        functools.partial(
            whole_kernel, num_doc, num_feat, subs, dir_subs, (2.0 / width_tile) ** 0.5
        ),
        out_shape=(shape((n, C), f32), shape((width_tile, C), f32)),
        in_specs=[anywhere] * 6,
        out_specs=(vmem, vmem),
        scratch_shapes=[
            pltpu.VMEM((2, num_doc * n, chunk), bf16),
            pltpu.VMEM((2, chunk, num_doc * n), bf16),
            pltpu.VMEM((n, n), f32),
            pltpu.VMEM((n, 3 * n), bf16),
            pltpu.VMEM((1, n), jnp.int32),
            pltpu.VMEM((1, n), f32),
            pltpu.VMEM((n, C), f32),
            pltpu.VMEM((n, C), f32),
            pltpu.VMEM((n, C), f32),
            dma((2,)),
            pltpu.VMEM((num_feat, num_doc, local_inputs, n), bf16),
            pltpu.VMEM((1, chunk), f32),
            pltpu.VMEM((1, chunk), f32),
            pltpu.VMEM((num_doc, input_rows, chunk), bf16),
            pltpu.VMEM((num_doc, n, n), f32),
            pltpu.VMEM((num_doc, n // 2 + 8, n), f32),
            pltpu.VMEM((num_doc, n // 2 + 8, n), f32),
            dma((2, 1)),
            dma((2, 1)),
            dma((2, dir_subs)),
            dma((2, 1)),
            dma,
            dma((3,)),
            pltpu.VMEM((ITERS, num_doc, n, C), jnp.int16),
            pltpu.VMEM((ITERS, num_doc, 1, C), f32),
            pltpu.VMEM((ITERS, n, C), f32),
            pltpu.VMEM((ITERS, num_feat, share, C), f32),
            pltpu.VMEM((ITERS, num_feat, 2, share, C), f32),
            pltpu.VMEM((rounds, num_doc, n, C), jnp.int16),
            pltpu.VMEM((rounds, num_doc, 1, C), f32),
            pltpu.VMEM((rounds, num_doc, n, C), jnp.int16),
            pltpu.VMEM((rounds, num_doc, 1, C), f32),
            pltpu.VMEM((rounds, num_doc * num_feat, 2, C), f32),
            pltpu.VMEM((chunk, C), f32),
            pltpu.VMEM((chunk, C), f32),
            pltpu.VMEM((chunk, C), f32),
            pltpu.VMEM((num_doc, subs, chunk // subs, C), jnp.int16),
            pltpu.VMEM((num_doc, subs, groups, 1, C), f32),
            dma((2, 2 * ITERS)),
            dma((2, ITERS)),
            dma((2, ITERS)),
            dma((2, 2 * rounds)),
            dma((2, rounds)),
            dma((2, 2)),
            dma((2, num_doc, subs)),
        ],
        compiler_params=pltpu.CompilerParams(
            collective_id=0, has_side_effects=True, vmem_limit_bytes=48 * 1024 * 1024
        ),
        name="admm",
    )(*[pltpu.with_memory_space_constraint(operand, pltpu.HBM) for operand in operands])
    return pl.pallas_call(
        hand_over,
        out_shape=(shape((n, C), f32), shape((width_tile, C), f32)),
        in_specs=[anywhere] * 2,
        out_specs=(anywhere,) * 2,
        scratch_shapes=[dma((2,))],
        compiler_params=pltpu.CompilerParams(vmem_limit_bytes=1024 * 1024),
        name="hand_over",
    )(margins, weights)


def solution(mesh):
    in_specs = (P("doc", "feat"), P("doc", "feat"), P("feat"), P("feat"), P("doc"), P("doc"))
    out_specs = (P("doc", None), P("feat", None))
    return jax.shard_map(
        per_device, mesh=mesh, in_specs=in_specs, out_specs=out_specs, check_vma=False
    )
```

```python
import functools

import jax
import jax.numpy as jnp
from jax import lax
from jax.experimental import pallas as pl
from jax.experimental.pallas import tpu as pltpu
from jax.sharding import PartitionSpec as P

C = 128
ITERS = 3
NEWTON = 3
LEVELS = 32767.0
INVERSE_STEPS = 7
DIR_SUBS = 2
HI = lax.Precision.HIGHEST
MESH = pl.DeviceIdType.MESH

shrink_level = 0.1
ratio_floor = 1e-06


def logistic_prox(target, signs, weight_ratio):
    current = target
    for newton_step in range(NEWTON):
        chance = 1.0 / (1.0 + jnp.exp(signs * current))
        gradient = current - target - weight_ratio * signs * chance
        current = current - gradient / (1.0 + weight_ratio * chance * (1.0 - chance))
    return current


def shrink_values(target, limit):
    return target - jnp.minimum(jnp.maximum(target, -limit), limit)


def cosine(angle):
    turns = jnp.floor(angle * 0.3183098861837907 + 0.5)
    rest = angle - turns * 3.140625
    rest = rest - turns * 9.67502593994140625e-4
    rest = rest - turns * 1.509957990978376432e-7
    odd = turns - 2.0 * jnp.floor(turns * 0.5)
    sq = rest * rest
    poly = 2.08767569878681e-9
    poly = poly * sq - 2.755731922398589e-7
    poly = poly * sq + 2.48015873015873e-5
    poly = poly * sq - 1.388888888888889e-3
    poly = poly * sq + 4.1666666666666664e-2
    poly = poly * sq - 0.5
    poly = poly * sq + 1.0
    return poly * (1.0 - 2.0 * odd)


def split(values):
    high = values.astype(jnp.bfloat16)
    return high, (values - high.astype(jnp.float32)).astype(jnp.bfloat16)


def split_dot(high, low, pair):
    both = jnp.dot(high, pair, preferred_element_type=jnp.float32)
    rest = jnp.dot(low, pair[:, :C], preferred_element_type=jnp.float32)
    return both[:, :C] + (both[:, C:] + rest)


def encode(values):
    largest = jnp.max(jnp.abs(values), axis=0, keepdims=True)
    steps = jnp.where(largest > 0.0, LEVELS / largest, 0.0)
    codes = jnp.floor(values * steps + 0.5).astype(jnp.int32).astype(jnp.int16)
    return codes, largest * (1.0 / LEVELS)


def decode(codes, steps):
    return codes.astype(jnp.int32).astype(jnp.float32) * steps


def remote(src, dst, send_sem, recv_sem, axis, peer):
    return pltpu.make_async_remote_copy(
        src_ref=src,
        dst_ref=dst,
        send_sem=send_sem,
        recv_sem=recv_sem,
        device_id={axis: peer},
        device_id_type=MESH,
    )


def greet(num_doc, num_feat):
    barrier = pltpu.get_barrier_semaphore()
    for axis, size in (("doc", num_doc), ("feat", num_feat)):
        me = lax.axis_index(axis)
        for k in range(1, size):
            pl.semaphore_signal(
                barrier, inc=1, device_id={axis: lax.rem(me + k, size)}, device_id_type=MESH
            )


def meet(num_doc, num_feat):
    pl.semaphore_wait(pltpu.get_barrier_semaphore(), num_doc + num_feat - 2)


class Gather:
    def __init__(self, sems, axis, size):
        self.sems, self.axis, self.size = sems, axis, size
        self.me = lax.axis_index(axis)

    def peers(self):
        return [lax.rem(self.me + k, self.size) for k in range(1, self.size)]

    def send(self, step, peer, src, dst):
        remote(src, dst, self.sems.at[0, step], self.sems.at[1, step], self.axis, peer).start()

    def all_of(self, step, rows):
        return remote(
            rows, rows, self.sems.at[0, step], self.sems.at[1, step], self.axis, self.peers()[0]
        )

    def rows(self, ref, *where):
        return ref.at[(*where, pl.ds(0, self.size - 1))]


def build_kernel(
    num_doc, num_feat, subs, scale, prepare,
    docs_ref, dir_ref, phase_hbm, amp_hbm,
    feat_ref, featt_ref, gram_ref,
    dpart, phase_ref, amp_ref, dirs, gsum, gsend, grecv,
    part_sems, row_sems, dir_sems, gram_sems, local_sem, table_sems,
):
    n = docs_ref.shape[1]
    chunk = dirs.shape[2]
    wide = chunk // subs
    me = lax.axis_index("doc")
    fme = lax.axis_index("feat")
    tables = [
        pltpu.make_async_copy(docs_ref, dpart.at[fme, me], table_sems.at[2]),
        pltpu.make_async_copy(phase_hbm.at[me], phase_ref, table_sems.at[0]),
        pltpu.make_async_copy(amp_hbm.at[me], amp_ref, table_sems.at[1]),
    ]
    for table in tables:
        table.start()
    local = pltpu.make_async_copy(
        dir_ref.at[:, pl.ds(pl.multiple_of(me * chunk, chunk), chunk)], dirs.at[me], local_sem
    )
    local.start()
    meet(num_doc, num_feat)
    ch_part = Gather(part_sems, "feat", num_feat)
    ch_row = Gather(row_sems, "doc", num_doc)
    ch_dir = Gather(dir_sems, "doc", num_doc)
    ch_gram = Gather(gram_sems, "doc", num_doc)
    for peer in ch_row.peers():
        ch_row.send(0, peer, docs_ref, dpart.at[fme, me])
    def send_dirs(s):
        for peer in ch_dir.peers():
            cols = pl.ds(pl.multiple_of(peer * chunk + s * wide, wide), wide)
            ch_dir.send(
                s, peer, dir_ref.at[:, cols], dirs.at[me, :, pl.ds(s * wide, wide)]
            )

    def dir_rows(s):
        return dirs.at[pl.ds(0, num_doc - 1), :, pl.ds(s * wide, wide)]

    for s in range(subs):
        send_dirs(s)
    tables[0].wait()
    ch_row.all_of(0, ch_row.rows(dpart, fme)).wait_recv()
    for peer in ch_part.peers():
        ch_part.send(0, peer, dpart.at[fme], dpart.at[fme])
    ch_part.all_of(0, ch_part.rows(dpart)).wait_recv()
    inputs = num_feat * docs_ref.shape[0]
    full = jnp.concatenate([dpart[:, i].reshape(inputs, n).T for i in range(num_doc)], axis=0)
    prepare()
    local.wait()
    for table in tables[1:]:
        table.wait()
    phase = phase_ref[...]
    amp = scale * amp_ref[...]
    for s in range(subs):
        cols = slice(s * wide, (s + 1) * wide)
        ch_dir.all_of(s, dir_rows(s)).wait_recv()
        piece = dirs[:, :, cols].reshape(full.shape[1], wide)
        angles = jnp.dot(full, piece, preferred_element_type=jnp.float32)
        feats = amp[:, cols] * cosine(angles + phase[:, cols])
        high, low = split(feats)
        feat_ref[0, :, cols], feat_ref[1, :, cols] = high, low
        for i in range(num_doc):
            block = slice(i * n, (i + 1) * n)
            both = lax.dot_general(
                high[block],
                jnp.concatenate([high[block], low[block]], axis=0),
                (((1,), (1,)), ((), ())),
                preferred_element_type=jnp.float32,
            )
            rest = lax.dot_general(
                low[block], high[block], (((1,), (1,)), ((), ())), preferred_element_type=jnp.float32
            )
            term = both[:, :n] + (both[:, n:] + rest)
            if s == 0:
                gsum[i] = term
            else:
                gsum[i] += term
        featt_ref[0, cols, :], featt_ref[1, cols, :] = split(feats.T)
    for k in range(1, num_doc + 1):
        peer = lax.rem(me + k, num_doc)
        gsend[peer] = pack_symmetric(gsum[peer])
        if k < num_doc:
            ch_gram.send(0, peer, gsend.at[peer], grecv.at[me])
    total = gsend[me]
    ch_gram.all_of(0, ch_gram.rows(grecv)).wait_recv()
    for peer in ch_gram.peers():
        total += grecv[peer]
    gram_ref[...] = unpack_symmetric(total)
    return [
        ch_row.all_of(0, ch_row.rows(dpart, fme)),
        ch_part.all_of(0, ch_part.rows(dpart)),
        ch_gram.all_of(0, ch_gram.rows(grecv)),
        *(ch_dir.all_of(s, dir_rows(s)) for s in range(subs)),
    ]


def pack_symmetric(values):
    half = values.shape[0] // 2
    rows = lax.broadcasted_iota(jnp.int32, (half, 2 * half), 0)
    lanes = lax.broadcasted_iota(jnp.int32, (half, 2 * half), 1)
    top, bottom = values[:half], values[half:]
    both = jnp.where(lanes <= rows + half, bottom, pltpu.roll(top, half, 1))
    diagonal = jnp.sum(jnp.where(rows == lanes, top, 0.0), axis=0, keepdims=True)
    return jnp.concatenate([both, jnp.broadcast_to(diagonal, (8, 2 * half))], axis=0)


def unpack_symmetric(packed):
    half = packed.shape[0] - 8
    rows = lax.broadcasted_iota(jnp.int32, (half, 2 * half), 0)
    lanes = lax.broadcasted_iota(jnp.int32, (half, 2 * half), 1)
    both, diagonal = packed[:half], packed[half : half + 1]
    flipped = jnp.concatenate([both, both], axis=0).T
    bottom = jnp.where(lanes <= rows + half, both, flipped[half:])
    corner = jnp.where(lanes > rows, pltpu.roll(both, half, 1), flipped[half:])
    corner = jnp.where(lanes == rows, diagonal, corner)
    return jnp.concatenate([jnp.where(lanes >= half, flipped[:half], corner), bottom], axis=0)


def three_left(values):
    high, low = split(values)
    return jnp.concatenate([high, high, low], axis=1)


def three_right(values):
    high, low = split(values)
    return jnp.concatenate([high, low, high], axis=0)


def three_dot(left, right):
    return jnp.dot(left, right, preferred_element_type=jnp.float32)


def invert(gram):
    n = gram.shape[0]
    rows = lax.broadcasted_iota(jnp.int32, (n, n), 0)
    lanes = lax.broadcasted_iota(jnp.int32, (n, n), 1)
    eye = jnp.where(rows == lanes, 1.0, 0.0)
    matrix = gram + eye
    bound = jnp.max(jnp.sum(jnp.abs(matrix), axis=0, keepdims=True), axis=1, keepdims=True)
    first = 2.0 / (1.0 + bound)
    error = (bound - 1.0) / (bound + 1.0)
    near = first * matrix
    guess = first * eye
    for k in range(INVERSE_STEPS):
        scale = 2.0 / (2.0 - error * error)
        error = 0.5 * error * error * scale
        if k == 0:
            moved = jnp.concatenate([first * near, three_dot(three_left(near), three_right(near))], axis=1)
        else:
            moved = three_dot(
                three_left(near), three_right(jnp.concatenate([guess, near], axis=1))
            )
        guess = scale * (2.0 * guess - moved[:, :n])
        near = scale * (2.0 * near - moved[:, n:])
    missing = eye - three_dot(three_left(matrix), three_right(guess))
    return guess + three_dot(three_left(guess), three_right(missing))


def fold(values):
    return jnp.sum(values.reshape(values.shape[0] // 8, 8, values.shape[1]), axis=0)


def admm_kernel(
    num_doc, num_feat, subs, begun,
    feat_ref, featt_ref, inv_ref, signs_ref, weight_ref, start_ref,
    m_ref, w_ref,
    solved, solved_step, part, yrecv, cbuf, psend, psend_step, precv, precv_step,
    norms, z, lastmove, lastlift, wcode, wstep,
    s_sems, y_sems, c_sems, p_sems, norm_sems, wsend_sems, w_sems,
):
    n = inv_ref.shape[0]
    chunk = z.shape[0]
    share = n // num_feat
    wide = chunk // subs
    me = lax.axis_index("doc")
    fme = lax.axis_index("feat")
    ch_s = Gather(s_sems, "doc", num_doc)
    ch_y = Gather(y_sems, "feat", num_feat)
    ch_c = Gather(c_sems, "feat", num_feat)
    ch_p = Gather(p_sems, "doc", num_doc)
    own = pl.ds(pl.multiple_of(fme * share, share), share)
    signs = signs_ref[own, :]
    weight = weight_ref[own, :]
    margins = start_ref[own, :]
    duals = jnp.zeros((share, C), jnp.float32)
    rho = jnp.ones((1, 1), jnp.float32)
    inv = inv_ref[...]
    target = start_ref[...] / num_feat
    residue = target
    growth = None

    mine = me * num_feat + fme
    others = [
        (lax.rem(me + i, num_doc), lax.rem(fme + j, num_feat))
        for i in reversed(range(num_doc))
        for j in range(num_feat)
        if i or j
    ]

    def norm_copy(step, target):
        row = norms.at[step, mine]
        return pltpu.make_async_remote_copy(
            src_ref=row,
            dst_ref=row,
            send_sem=norm_sems.at[0, step],
            recv_sem=norm_sems.at[1, step],
            device_id={"doc": target[0], "feat": target[1]},
            device_id_type=MESH,
        )

    def norm_all(step):
        rows = norms.at[step, pl.ds(0, len(others))]
        return remote(rows, rows, norm_sems.at[0, step], norm_sems.at[1, step], "doc", others[0][0])

    groups = wstep.shape[2]
    rows_per = wide // groups

    def w_copy(direction, src, s, peer):
        return [
            remote(
                ref.at[src, s], ref.at[src, s],
                wsend_sems.at[direction, k], w_sems.at[k, src, s], "doc", peer,
            )
            for k, ref in enumerate((wcode, wstep))
        ]

    def w_write(src, s):
        for g in range(groups):
            first = pl.multiple_of(src * chunk + s * wide + g * rows_per, rows_per)
            piece = wcode[src, s, g * rows_per : (g + 1) * rows_per, :]
            w_ref[pl.ds(first, rows_per), :] = decode(piece, wstep[src, s, g])

    def s_all(step):
        return [
            ch_s.all_of(2 * step + k, ch_s.rows(ref, step))
            for k, ref in enumerate((solved, solved_step))
        ]

    def p_all(step):
        return [
            ch_p.all_of(2 * step + k, ch_p.rows(ref, step))
            for k, ref in enumerate((precv, precv_step))
        ]

    def send_margins(step):
        for peer in ch_c.peers():
            ch_c.send(step, peer, cbuf.at[step, fme], cbuf.at[step, fme])

    for step in range(ITERS):
        last = step + 1 == ITERS
        if step == 0:
            answer = three_dot(inv, three_right(residue))
        applied = residue - answer
        new_part = target - answer
        solved[step, me], solved_step[step, me] = encode(answer)
        part[step] = new_part
        for peer in ch_s.peers():
            ch_s.send(2 * step, peer, solved.at[step, me], solved.at[step, me])
            ch_s.send(2 * step + 1, peer, solved_step.at[step, me], solved_step.at[step, me])
        for peer in ch_y.peers():
            rows = pl.ds(pl.multiple_of(peer * share, share), share)
            ch_y.send(step, peer, part.at[step, rows, :], yrecv.at[step, fme])
        yrecv[step, fme] = part[step, own, :]
        ch_y.all_of(step, ch_y.rows(yrecv, step)).wait_recv()
        sums = yrecv[step, 0]
        for k in range(1, num_feat):
            sums += yrecv[step, k]
        old_margins = margins
        margins = logistic_prox(sums + duals, signs, weight / rho)
        duals = duals + sums - margins
        cbuf[step, fme, 0] = margins if last else (margins - sums) / num_feat
        cbuf[step, fme, 1] = duals / num_feat
        send_margins(step)
        for copy in s_all(step):
            copy.wait_recv()
        everything = jnp.concatenate(
            split(decode(solved[step], solved_step[step]).reshape(num_doc * n, C)), axis=1
        )
        limit = shrink_level / (rho * num_doc)
        if not last:
            gap = fold((sums - margins) ** 2) if share > 8 else (sums - margins) ** 2
            shift = (
                fold((margins - old_margins) ** 2) if share > 8 else (margins - old_margins) ** 2
            )
            if step == 0:
                d_answer, d_applied = answer, applied
            else:
                d_answer = answer - last_answer / growth
                d_applied = applied - last_applied / growth
            primal = gap + fold(d_answer * d_applied)
            dual = shift
        for s in range(subs if last else 1):
            rows = slice(s * wide, (s + 1) * wide) if last else slice(0, chunk)
            lift = split_dot(featt_ref[0, rows, :], featt_ref[1, rows, :], everything)
            if step == 0:
                fresh = shrink_values(lift / num_doc, limit)
                move = -fresh
                d_move, d_lift = move, lift
            else:
                old = z[rows, :]
                fresh = shrink_values(old + lift / num_doc, limit)
                if not last:
                    move = old - fresh
                    d_move = move - lastmove[rows, :] / growth
                    d_lift = lift - lastlift[rows, :] / growth
            if last:
                for g in range(groups):
                    piece = slice(g * rows_per, (g + 1) * rows_per)
                    wcode[me, s, piece, :], wstep[me, s, g] = encode(num_feat * fresh[piece])

                @pl.when(me + 1 < num_doc)
                def _(s=s):
                    for copy in w_copy(0, me, s, me + 1):
                        copy.start()

                @pl.when(me >= 1)
                def _(s=s):
                    for copy in w_copy(1, me, s, me - 1):
                        copy.start()

                w_write(me, s)
            else:
                z[rows, :] = fresh
                lastmove[rows, :] = move
                lastlift[rows, :] = lift
                primal += fold(num_doc * d_move * d_move + 2.0 * d_move * d_lift)
                dual += num_doc * fold(move * move)
        if last:
            break
        norms[step, mine, 0:1] = jnp.sum(primal, axis=0, keepdims=True)
        norms[step, mine, 1:2] = jnp.sum(dual, axis=0, keepdims=True)
        for target in others:
            norm_copy(step, target).start()
        weights = jnp.concatenate(split(z[...]), axis=1)
        for k in range(1, num_doc + 1):
            peer = lax.rem(me + k, num_doc)
            block = pl.ds(pl.multiple_of(peer * n, n), n)
            product = split_dot(feat_ref[0, block, :], feat_ref[1, block, :], weights)
            if k < num_doc:
                psend[step, k - 1], psend_step[step, k - 1] = encode(product)
                ch_p.send(2 * step, peer, psend.at[step, k - 1], precv.at[step, me])
                ch_p.send(2 * step + 1, peer, psend_step.at[step, k - 1], precv_step.at[step, me])
        last_answer, last_applied = answer, applied
        ch_c.all_of(step, ch_c.rows(cbuf, step)).wait_recv()
        margins_part = cbuf[step, :, 0].reshape(n, C)
        duals_part = cbuf[step, :, 1].reshape(n, C)
        for copy in p_all(step):
            copy.wait_recv()
        for peer in ch_p.peers():
            product += decode(precv[step, peer], precv_step[step, peer])
        kept = new_part + margins_part - product
        shrunk = applied - product - duals_part if step == 0 else (
            old_product - product + applied - duals_part
        )
        old_product = product
        both = three_dot(inv, three_right(jnp.concatenate([kept, shrunk], axis=1)))
        norm_all(step).wait_recv()
        sums_of = jnp.sum(jnp.sum(norms[step], axis=0), axis=1, keepdims=True)
        primal = jnp.maximum(sums_of[0:1], 0.0)
        dual = sums_of[1:2]
        growth = jnp.sqrt(
            jnp.sqrt((primal + ratio_floor) / (rho * rho * dual + ratio_floor))
        )
        rho = rho * growth
        shrink = 1.0 / growth
        duals = duals * shrink
        target = new_part + margins_part - duals_part * shrink
        residue = kept + shrunk * shrink
        answer = both[:, :C] + both[:, C:] * shrink
    def w_sent(direction, count):
        for k, ref in enumerate((wcode, wstep)):
            rows = ref.at[pl.ds(0, count)]
            remote(
                rows, rows, wsend_sems.at[direction, k], w_sems.at[k, 0, 0], "doc", lax.rem(me + 1, num_doc)
            ).wait_send()

    for step in range(ITERS):
        begun += s_all(step)
        if step + 1 < ITERS:
            begun += [*p_all(step), norm_all(step)]
    for copy in begun:
        copy.wait_send()
    for hop in range(1, num_doc):
        if hop == min(2, num_doc - 1):
            ch_c.all_of(ITERS - 1, ch_c.rows(cbuf, ITERS - 1)).wait_recv()
            m_ref[...] = cbuf[ITERS - 1, :, 0].reshape(n, C)
            for step in range(ITERS):
                ch_y.all_of(step, ch_y.rows(yrecv, step)).wait_send()
                ch_c.all_of(step, ch_c.rows(cbuf, step)).wait_send()
        for s in range(subs):

            @pl.when(me >= hop)
            def _(hop=hop, s=s):
                for copy in w_copy(0, me - hop, s, me):
                    copy.wait_recv()

                @pl.when(me + 1 < num_doc)
                def _():
                    for copy in w_copy(0, me - hop, s, me + 1):
                        copy.start()

                w_write(me - hop, s)

            @pl.when(me + hop < num_doc)
            def _(hop=hop, s=s):
                for copy in w_copy(1, me + hop, s, me):
                    copy.wait_recv()

                @pl.when(me >= 1)
                def _():
                    for copy in w_copy(1, me + hop, s, me - 1):
                        copy.start()

                w_write(me + hop, s)

    for count in range(1, num_doc):

        @pl.when(me + 1 == count)
        def _(count=count):
            w_sent(0, count)

        @pl.when(me + count == num_doc)
        def _(count=count):
            w_sent(1, count)


def whole_kernel(
    num_doc, num_feat, subs, dir_subs, scale,
    docs_ref, dir_ref, phase_hbm, amp_hbm, lab_hbm, dw_hbm,
    m_ref, w_ref,
    feat_ref, featt_ref, gram_ref, inv_ref,
    lab_ref, dw_ref, signs_ref, weight_ref, start_ref, small_sems,
    *scratch,
):
    n = gram_ref.shape[0]
    greet(num_doc, num_feat)
    smalls = [
        pltpu.make_async_copy(lab_hbm, lab_ref, small_sems.at[0]),
        pltpu.make_async_copy(dw_hbm, dw_ref, small_sems.at[1]),
    ]
    for small in smalls:
        small.start()

    def prepare():
        for small in smalls:
            small.wait()
        classes = lax.broadcasted_iota(jnp.int32, (n, C), 1).astype(jnp.float32)
        spread = jnp.broadcast_to(lab_ref[...].astype(jnp.float32), (C, n)).T
        weight = jnp.broadcast_to(dw_ref[...], (C, n)).T
        signs = jnp.where(spread == classes, 1.0, -1.0)
        signs_ref[...] = signs
        weight_ref[...] = weight
        start_ref[...] = logistic_prox(jnp.zeros((n, C), jnp.float32), signs, weight)

    begun = build_kernel(
        num_doc, num_feat, dir_subs, scale, prepare,
        docs_ref, dir_ref, phase_hbm, amp_hbm, feat_ref, featt_ref, gram_ref, *scratch[:13],
    )
    inv_ref[...] = three_left(invert(gram_ref[...]))
    admm_kernel(
        num_doc, num_feat, subs, begun,
        feat_ref, featt_ref, inv_ref, signs_ref, weight_ref, start_ref, m_ref, w_ref,
        *scratch[13:],
    )


def hand_over(margins_ref, weights_ref, m_ref, w_ref, sems):
    copies = [
        pltpu.make_async_copy(margins_ref, m_ref, sems.at[0]),
        pltpu.make_async_copy(weights_ref, w_ref, sems.at[1]),
    ]
    for copy in copies:
        copy.start()
    for copy in copies:
        copy.wait()


def per_device(documents, directions, phase, amplitude, doc_weight, labels):
    n, local_inputs = documents.shape
    input_rows, width_tile = directions.shape
    num_feat = lax.axis_size("feat")
    num_doc = lax.axis_size("doc")
    chunk = width_tile // num_doc
    subs = max(1, min(4, chunk // 128))
    dir_subs = max(1, min(DIR_SUBS, chunk // 128))
    share = n // num_feat
    f32, bf16 = jnp.float32, jnp.bfloat16
    vmem = pl.BlockSpec(memory_space=pltpu.VMEM)
    dma = pltpu.SemaphoreType.DMA
    shape = jax.ShapeDtypeStruct
    rounds = ITERS - 1
    anywhere = pl.BlockSpec(memory_space=pl.ANY)
    groups = max(1, chunk // subs // n)
    operands = (
        documents.T,
        directions,
        phase.reshape(num_doc, 1, chunk),
        amplitude.reshape(num_doc, 1, chunk),
        labels.reshape(1, n),
        doc_weight.reshape(1, n),
    )
    margins, weights = pl.pallas_call(
        functools.partial(
            whole_kernel, num_doc, num_feat, subs, dir_subs, (2.0 / width_tile) ** 0.5
        ),
        out_shape=(shape((n, C), f32), shape((width_tile, C), f32)),
        in_specs=[anywhere] * 6,
        out_specs=(vmem, vmem),
        scratch_shapes=[
            pltpu.VMEM((2, num_doc * n, chunk), bf16),
            pltpu.VMEM((2, chunk, num_doc * n), bf16),
            pltpu.VMEM((n, n), f32),
            pltpu.VMEM((n, 3 * n), bf16),
            pltpu.VMEM((1, n), jnp.int32),
            pltpu.VMEM((1, n), f32),
            pltpu.VMEM((n, C), f32),
            pltpu.VMEM((n, C), f32),
            pltpu.VMEM((n, C), f32),
            dma((2,)),
            pltpu.VMEM((num_feat, num_doc, local_inputs, n), bf16),
            pltpu.VMEM((1, chunk), f32),
            pltpu.VMEM((1, chunk), f32),
            pltpu.VMEM((num_doc, input_rows, chunk), bf16),
            pltpu.VMEM((num_doc, n, n), f32),
            pltpu.VMEM((num_doc, n // 2 + 8, n), f32),
            pltpu.VMEM((num_doc, n // 2 + 8, n), f32),
            dma((2, 1)),
            dma((2, 1)),
            dma((2, dir_subs)),
            dma((2, 1)),
            dma,
            dma((3,)),
            pltpu.VMEM((ITERS, num_doc, n, C), jnp.int16),
            pltpu.VMEM((ITERS, num_doc, 1, C), f32),
            pltpu.VMEM((ITERS, n, C), f32),
            pltpu.VMEM((ITERS, num_feat, share, C), f32),
            pltpu.VMEM((ITERS, num_feat, 2, share, C), f32),
            pltpu.VMEM((rounds, num_doc, n, C), jnp.int16),
            pltpu.VMEM((rounds, num_doc, 1, C), f32),
            pltpu.VMEM((rounds, num_doc, n, C), jnp.int16),
            pltpu.VMEM((rounds, num_doc, 1, C), f32),
            pltpu.VMEM((rounds, num_doc * num_feat, 2, C), f32),
            pltpu.VMEM((chunk, C), f32),
            pltpu.VMEM((chunk, C), f32),
            pltpu.VMEM((chunk, C), f32),
            pltpu.VMEM((num_doc, subs, chunk // subs, C), jnp.int16),
            pltpu.VMEM((num_doc, subs, groups, 1, C), f32),
            dma((2, 2 * ITERS)),
            dma((2, ITERS)),
            dma((2, ITERS)),
            dma((2, 2 * rounds)),
            dma((2, rounds)),
            dma((2, 2)),
            dma((2, num_doc, subs)),
        ],
        compiler_params=pltpu.CompilerParams(
            collective_id=0, has_side_effects=True, vmem_limit_bytes=48 * 1024 * 1024
        ),
        name="admm",
    )(*[pltpu.with_memory_space_constraint(operand, pltpu.HBM) for operand in operands])
    return pl.pallas_call(
        hand_over,
        out_shape=(shape((n, C), f32), shape((width_tile, C), f32)),
        in_specs=[anywhere] * 2,
        out_specs=(anywhere,) * 2,
        scratch_shapes=[dma((2,))],
        compiler_params=pltpu.CompilerParams(vmem_limit_bytes=1024 * 1024),
        name="hand_over",
    )(margins, weights)


def solution(mesh):
    in_specs = (P("doc", "feat"), P("doc", "feat"), P("feat"), P("feat"), P("doc"), P("doc"))
    out_specs = (P("doc", None), P("feat", None))
    return jax.shard_map(
        per_device, mesh=mesh, in_specs=in_specs, out_specs=out_specs, check_vma=False
    )
```

```python
import functools

import jax
import jax.numpy as jnp
from jax import lax
from jax.experimental import pallas as pl
from jax.experimental.pallas import tpu as pltpu
from jax.sharding import PartitionSpec as P

C = 128
ITERS = 3
NEWTON = 3
LEVELS = 32767.0
INVERSE_STEPS = 7
DIR_SUBS = 2
HI = lax.Precision.HIGHEST
MESH = pl.DeviceIdType.MESH

shrink_level = 0.1
ratio_floor = 1e-06


def logistic_prox(target, signs, weight_ratio):
    current = target
    for newton_step in range(NEWTON):
        chance = 1.0 / (1.0 + jnp.exp(signs * current))
        gradient = current - target - weight_ratio * signs * chance
        current = current - gradient / (1.0 + weight_ratio * chance * (1.0 - chance))
    return current


def shrink_values(target, limit):
    return target - jnp.minimum(jnp.maximum(target, -limit), limit)


def cosine(angle):
    turns = jnp.floor(angle * 0.3183098861837907 + 0.5)
    rest = angle - turns * 3.140625
    rest = rest - turns * 9.67502593994140625e-4
    rest = rest - turns * 1.509957990978376432e-7
    odd = turns - 2.0 * jnp.floor(turns * 0.5)
    sq = rest * rest
    poly = 2.08767569878681e-9
    poly = poly * sq - 2.755731922398589e-7
    poly = poly * sq + 2.48015873015873e-5
    poly = poly * sq - 1.388888888888889e-3
    poly = poly * sq + 4.1666666666666664e-2
    poly = poly * sq - 0.5
    poly = poly * sq + 1.0
    return poly * (1.0 - 2.0 * odd)


def split(values):
    high = values.astype(jnp.bfloat16)
    return high, (values - high.astype(jnp.float32)).astype(jnp.bfloat16)


def split_dot(high, low, pair):
    both = jnp.dot(high, pair, preferred_element_type=jnp.float32)
    rest = jnp.dot(low, pair[:, :C], preferred_element_type=jnp.float32)
    return both[:, :C] + (both[:, C:] + rest)


def encode(values):
    largest = jnp.max(jnp.abs(values), axis=0, keepdims=True)
    steps = jnp.where(largest > 0.0, LEVELS / largest, 0.0)
    codes = jnp.round(values * steps).astype(jnp.int32).astype(jnp.int16)
    return codes, largest * (1.0 / LEVELS)


def decode(codes, steps):
    return codes.astype(jnp.int32).astype(jnp.float32) * steps


def remote(src, dst, send_sem, recv_sem, axis, peer):
    return pltpu.make_async_remote_copy(
        src_ref=src,
        dst_ref=dst,
        send_sem=send_sem,
        recv_sem=recv_sem,
        device_id={axis: peer},
        device_id_type=MESH,
    )


def greet(num_doc, num_feat):
    barrier = pltpu.get_barrier_semaphore()
    for axis, size in (("doc", num_doc), ("feat", num_feat)):
        me = lax.axis_index(axis)
        for k in range(1, size):
            pl.semaphore_signal(
                barrier, inc=1, device_id={axis: lax.rem(me + k, size)}, device_id_type=MESH
            )
    pl.semaphore_wait(barrier, num_doc + num_feat - 2)


class Gather:
    def __init__(self, sems, axis, size):
        self.sems, self.axis, self.size = sems, axis, size
        self.me = lax.axis_index(axis)

    def peers(self):
        return [lax.rem(self.me + k, self.size) for k in range(1, self.size)]

    def send(self, step, peer, src, dst):
        remote(src, dst, self.sems.at[0, step], self.sems.at[1, step], self.axis, peer).start()

    def all_of(self, step, rows):
        return remote(
            rows, rows, self.sems.at[0, step], self.sems.at[1, step], self.axis, self.peers()[0]
        )

    def rows(self, ref, *where):
        return ref.at[(*where, pl.ds(0, self.size - 1))]


def build_kernel(
    num_doc, num_feat, subs, scale, prepare,
    docs_ref, dir_ref, phase_hbm, amp_hbm,
    feat_ref, featt_ref, gram_ref,
    dpart, phase_ref, amp_ref, dirs, gsum, gsend, grecv,
    part_sems, row_sems, dir_sems, gram_sems, local_sem, table_sems,
):
    n = docs_ref.shape[1]
    chunk = dirs.shape[2]
    wide = chunk // subs
    me = lax.axis_index("doc")
    fme = lax.axis_index("feat")
    tables = [
        pltpu.make_async_copy(docs_ref, dpart.at[fme, me], table_sems.at[2]),
        pltpu.make_async_copy(phase_hbm.at[me], phase_ref, table_sems.at[0]),
        pltpu.make_async_copy(amp_hbm.at[me], amp_ref, table_sems.at[1]),
    ]
    for table in tables:
        table.start()
    local = pltpu.make_async_copy(
        dir_ref.at[:, pl.ds(pl.multiple_of(me * chunk, chunk), chunk)], dirs.at[me], local_sem
    )
    local.start()
    greet(num_doc, num_feat)
    ch_part = Gather(part_sems, "feat", num_feat)
    ch_row = Gather(row_sems, "doc", num_doc)
    ch_dir = Gather(dir_sems, "doc", num_doc)
    ch_gram = Gather(gram_sems, "doc", num_doc)
    for peer in ch_row.peers():
        ch_row.send(0, peer, docs_ref, dpart.at[fme, me])
    def send_dirs(s):
        for peer in ch_dir.peers():
            cols = pl.ds(pl.multiple_of(peer * chunk + s * wide, wide), wide)
            ch_dir.send(
                s, peer, dir_ref.at[:, cols], dirs.at[me, :, pl.ds(s * wide, wide)]
            )

    def dir_rows(s):
        return dirs.at[pl.ds(0, num_doc - 1), :, pl.ds(s * wide, wide)]

    for s in range(subs):
        send_dirs(s)
    tables[0].wait()
    ch_row.all_of(0, ch_row.rows(dpart, fme)).wait_recv()
    for peer in ch_part.peers():
        ch_part.send(0, peer, dpart.at[fme], dpart.at[fme])
    ch_part.all_of(0, ch_part.rows(dpart)).wait_recv()
    inputs = num_feat * docs_ref.shape[0]
    full = jnp.concatenate([dpart[:, i].reshape(inputs, n).T for i in range(num_doc)], axis=0)
    prepare()
    local.wait()
    for table in tables[1:]:
        table.wait()
    phase = phase_ref[...]
    amp = scale * amp_ref[...]
    for s in range(subs):
        cols = slice(s * wide, (s + 1) * wide)
        ch_dir.all_of(s, dir_rows(s)).wait_recv()
        piece = dirs[:, :, cols].reshape(full.shape[1], wide)
        angles = jnp.dot(full, piece, preferred_element_type=jnp.float32)
        feats = amp[:, cols] * cosine(angles + phase[:, cols])
        high, low = split(feats)
        feat_ref[0, :, cols], feat_ref[1, :, cols] = high, low
        for i in range(num_doc):
            block = slice(i * n, (i + 1) * n)
            both = lax.dot_general(
                high[block],
                jnp.concatenate([high[block], low[block]], axis=0),
                (((1,), (1,)), ((), ())),
                preferred_element_type=jnp.float32,
            )
            rest = lax.dot_general(
                low[block], high[block], (((1,), (1,)), ((), ())), preferred_element_type=jnp.float32
            )
            term = both[:, :n] + (both[:, n:] + rest)
            if s == 0:
                gsum[i] = term
            else:
                gsum[i] += term
        featt_ref[0, cols, :], featt_ref[1, cols, :] = split(feats.T)
    for k in range(1, num_doc + 1):
        peer = lax.rem(me + k, num_doc)
        gsend[peer] = pack_symmetric(gsum[peer])
        if k < num_doc:
            ch_gram.send(0, peer, gsend.at[peer], grecv.at[me])
    total = gsend[me]
    ch_gram.all_of(0, ch_gram.rows(grecv)).wait_recv()
    for peer in ch_gram.peers():
        total += grecv[peer]
    gram_ref[...] = unpack_symmetric(total)
    return [
        ch_row.all_of(0, ch_row.rows(dpart, fme)),
        ch_part.all_of(0, ch_part.rows(dpart)),
        ch_gram.all_of(0, ch_gram.rows(grecv)),
        *(ch_dir.all_of(s, dir_rows(s)) for s in range(subs)),
    ]


def pack_symmetric(values):
    half = values.shape[0] // 2
    rows = lax.broadcasted_iota(jnp.int32, (half, 2 * half), 0)
    lanes = lax.broadcasted_iota(jnp.int32, (half, 2 * half), 1)
    top, bottom = values[:half], values[half:]
    both = jnp.where(lanes <= rows + half, bottom, pltpu.roll(top, half, 1))
    diagonal = jnp.sum(jnp.where(rows == lanes, top, 0.0), axis=0, keepdims=True)
    return jnp.concatenate([both, jnp.broadcast_to(diagonal, (8, 2 * half))], axis=0)


def unpack_symmetric(packed):
    half = packed.shape[0] - 8
    rows = lax.broadcasted_iota(jnp.int32, (half, 2 * half), 0)
    lanes = lax.broadcasted_iota(jnp.int32, (half, 2 * half), 1)
    both, diagonal = packed[:half], packed[half : half + 1]
    flipped = jnp.concatenate([both, both], axis=0).T
    bottom = jnp.where(lanes <= rows + half, both, flipped[half:])
    corner = jnp.where(lanes > rows, pltpu.roll(both, half, 1), flipped[half:])
    corner = jnp.where(lanes == rows, diagonal, corner)
    return jnp.concatenate([jnp.where(lanes >= half, flipped[:half], corner), bottom], axis=0)


def three_left(values):
    high, low = split(values)
    return jnp.concatenate([high, high, low], axis=1)


def three_right(values):
    high, low = split(values)
    return jnp.concatenate([high, low, high], axis=0)


def three_dot(left, right):
    return jnp.dot(left, right, preferred_element_type=jnp.float32)


def invert(gram):
    n = gram.shape[0]
    rows = lax.broadcasted_iota(jnp.int32, (n, n), 0)
    lanes = lax.broadcasted_iota(jnp.int32, (n, n), 1)
    eye = jnp.where(rows == lanes, 1.0, 0.0)
    matrix = gram + eye
    bound = jnp.max(jnp.sum(jnp.abs(matrix), axis=0, keepdims=True), axis=1, keepdims=True)
    first = 2.0 / (1.0 + bound)
    error = (bound - 1.0) / (bound + 1.0)
    near = first * matrix
    guess = first * eye
    for k in range(INVERSE_STEPS):
        scale = 2.0 / (2.0 - error * error)
        error = 0.5 * error * error * scale
        if k == 0:
            moved = jnp.concatenate([first * near, three_dot(three_left(near), three_right(near))], axis=1)
        else:
            moved = three_dot(
                three_left(near), three_right(jnp.concatenate([guess, near], axis=1))
            )
        guess = scale * (2.0 * guess - moved[:, :n])
        near = scale * (2.0 * near - moved[:, n:])
    missing = eye - jnp.dot(matrix, guess, precision=HI)
    return guess + three_dot(three_left(guess), three_right(missing))


def fold(values):
    return jnp.sum(values.reshape(values.shape[0] // 8, 8, values.shape[1]), axis=0)


def admm_kernel(
    num_doc, num_feat, subs, begun,
    feat_ref, featt_ref, inv_ref, signs_ref, weight_ref, start_ref,
    m_ref, w_ref,
    solved, solved_step, part, yrecv, cbuf, psend, psend_step, precv, precv_step,
    norms, z, lastmove, lastlift, wcode, wstep,
    s_sems, y_sems, c_sems, p_sems, norm_sems, wsend_sems, w_sems,
):
    n = inv_ref.shape[0]
    chunk = z.shape[0]
    share = n // num_feat
    wide = chunk // subs
    me = lax.axis_index("doc")
    fme = lax.axis_index("feat")
    ch_s = Gather(s_sems, "doc", num_doc)
    ch_y = Gather(y_sems, "feat", num_feat)
    ch_c = Gather(c_sems, "feat", num_feat)
    ch_p = Gather(p_sems, "doc", num_doc)
    own = pl.ds(pl.multiple_of(fme * share, share), share)
    signs = signs_ref[own, :]
    weight = weight_ref[own, :]
    margins = start_ref[own, :]
    duals = jnp.zeros((share, C), jnp.float32)
    rho = jnp.ones((1, 1), jnp.float32)
    inv = inv_ref[...]
    target = start_ref[...] / num_feat
    residue = target
    growth = None

    mine = me * num_feat + fme
    others = [
        (lax.rem(me + i, num_doc), lax.rem(fme + j, num_feat))
        for i in range(num_doc)
        for j in range(num_feat)
        if i or j
    ]

    def norm_copy(step, target):
        row = norms.at[step, mine]
        return pltpu.make_async_remote_copy(
            src_ref=row,
            dst_ref=row,
            send_sem=norm_sems.at[0, step],
            recv_sem=norm_sems.at[1, step],
            device_id={"doc": target[0], "feat": target[1]},
            device_id_type=MESH,
        )

    def norm_all(step):
        rows = norms.at[step, pl.ds(0, len(others))]
        return remote(rows, rows, norm_sems.at[0, step], norm_sems.at[1, step], "doc", others[-1][0])

    groups = wstep.shape[2]
    rows_per = wide // groups

    def w_copy(direction, src, s, peer):
        return [
            remote(
                ref.at[src, s], ref.at[src, s],
                wsend_sems.at[direction, k], w_sems.at[k, src, s], "doc", peer,
            )
            for k, ref in enumerate((wcode, wstep))
        ]

    def w_write(src, s):
        for g in range(groups):
            first = pl.multiple_of(src * chunk + s * wide + g * rows_per, rows_per)
            piece = wcode[src, s, g * rows_per : (g + 1) * rows_per, :]
            w_ref[pl.ds(first, rows_per), :] = decode(piece, wstep[src, s, g])

    def s_all(step):
        return [
            ch_s.all_of(2 * step + k, ch_s.rows(ref, step))
            for k, ref in enumerate((solved, solved_step))
        ]

    def p_all(step):
        return [
            ch_p.all_of(2 * step + k, ch_p.rows(ref, step))
            for k, ref in enumerate((precv, precv_step))
        ]

    def send_margins(step):
        for peer in ch_c.peers():
            ch_c.send(step, peer, cbuf.at[step, fme], cbuf.at[step, fme])

    for step in range(ITERS):
        last = step + 1 == ITERS
        if step == 0:
            answer = three_dot(inv, three_right(residue))
        applied = residue - answer
        new_part = target - answer
        solved[step, me], solved_step[step, me] = encode(answer)
        part[step] = new_part
        for peer in ch_s.peers():
            ch_s.send(2 * step, peer, solved.at[step, me], solved.at[step, me])
            ch_s.send(2 * step + 1, peer, solved_step.at[step, me], solved_step.at[step, me])
        for peer in ch_y.peers():
            rows = pl.ds(pl.multiple_of(peer * share, share), share)
            ch_y.send(step, peer, part.at[step, rows, :], yrecv.at[step, fme])
        yrecv[step, fme] = part[step, own, :]
        ch_y.all_of(step, ch_y.rows(yrecv, step)).wait_recv()
        sums = yrecv[step, 0]
        for k in range(1, num_feat):
            sums += yrecv[step, k]
        old_margins = margins
        margins = logistic_prox(sums + duals, signs, weight / rho)
        duals = duals + sums - margins
        cbuf[step, fme, 0] = margins if last else (margins - sums) / num_feat
        cbuf[step, fme, 1] = duals / num_feat
        send_margins(step)
        for copy in s_all(step):
            copy.wait_recv()
        everything = jnp.concatenate(
            split(decode(solved[step], solved_step[step]).reshape(num_doc * n, C)), axis=1
        )
        limit = shrink_level / (rho * num_doc)
        if not last:
            gap = fold((sums - margins) ** 2) if share > 8 else (sums - margins) ** 2
            shift = (
                fold((margins - old_margins) ** 2) if share > 8 else (margins - old_margins) ** 2
            )
            if step == 0:
                d_answer, d_applied = answer, applied
            else:
                d_answer = answer - last_answer / growth
                d_applied = applied - last_applied / growth
            primal = gap + fold(d_answer * d_applied)
            dual = shift
        for s in range(subs if last else 1):
            rows = slice(s * wide, (s + 1) * wide) if last else slice(0, chunk)
            lift = split_dot(featt_ref[0, rows, :], featt_ref[1, rows, :], everything)
            if step == 0:
                fresh = shrink_values(lift / num_doc, limit)
                move = -fresh
                d_move, d_lift = move, lift
            else:
                old = z[rows, :]
                fresh = shrink_values(old + lift / num_doc, limit)
                if not last:
                    move = old - fresh
                    d_move = move - lastmove[rows, :] / growth
                    d_lift = lift - lastlift[rows, :] / growth
            if last:
                for g in range(groups):
                    piece = slice(g * rows_per, (g + 1) * rows_per)
                    wcode[me, s, piece, :], wstep[me, s, g] = encode(num_feat * fresh[piece])

                @pl.when(me + 1 < num_doc)
                def _(s=s):
                    for copy in w_copy(0, me, s, me + 1):
                        copy.start()

                @pl.when(me >= 1)
                def _(s=s):
                    for copy in w_copy(1, me, s, me - 1):
                        copy.start()

                w_write(me, s)
            else:
                z[rows, :] = fresh
                lastmove[rows, :] = move
                lastlift[rows, :] = lift
                primal += fold(num_doc * d_move * d_move + 2.0 * d_move * d_lift)
                dual += num_doc * fold(move * move)
        if last:
            break
        norms[step, mine, 0:1] = jnp.sum(primal, axis=0, keepdims=True)
        norms[step, mine, 1:2] = jnp.sum(dual, axis=0, keepdims=True)
        for target in others:
            norm_copy(step, target).start()
        weights = jnp.concatenate(split(z[...]), axis=1)
        for k in range(1, num_doc + 1):
            peer = lax.rem(me + k, num_doc)
            block = pl.ds(pl.multiple_of(peer * n, n), n)
            product = split_dot(feat_ref[0, block, :], feat_ref[1, block, :], weights)
            if k < num_doc:
                psend[step, k - 1], psend_step[step, k - 1] = encode(product)
                ch_p.send(2 * step, peer, psend.at[step, k - 1], precv.at[step, me])
                ch_p.send(2 * step + 1, peer, psend_step.at[step, k - 1], precv_step.at[step, me])
        last_answer, last_applied = answer, applied
        ch_c.all_of(step, ch_c.rows(cbuf, step)).wait_recv()
        margins_part = cbuf[step, :, 0].reshape(n, C)
        duals_part = cbuf[step, :, 1].reshape(n, C)
        for copy in p_all(step):
            copy.wait_recv()
        for peer in ch_p.peers():
            product += decode(precv[step, peer], precv_step[step, peer])
        kept = new_part + margins_part - product
        shrunk = applied - product - duals_part if step == 0 else (
            old_product - product + applied - duals_part
        )
        old_product = product
        both = three_dot(inv, three_right(jnp.concatenate([kept, shrunk], axis=1)))
        norm_all(step).wait_recv()
        sums_of = jnp.sum(jnp.sum(norms[step], axis=0), axis=1, keepdims=True)
        primal = jnp.maximum(sums_of[0:1], 0.0)
        dual = sums_of[1:2]
        growth = jnp.sqrt(
            jnp.sqrt((primal + ratio_floor) / (rho * rho * dual + ratio_floor))
        )
        rho = rho * growth
        shrink = 1.0 / growth
        duals = duals * shrink
        target = new_part + margins_part - duals_part * shrink
        residue = kept + shrunk * shrink
        answer = both[:, :C] + both[:, C:] * shrink
    def w_sent(direction, count):
        for k, ref in enumerate((wcode, wstep)):
            rows = ref.at[pl.ds(0, count)]
            remote(
                rows, rows, wsend_sems.at[direction, k], w_sems.at[k, 0, 0], "doc", lax.rem(me + 1, num_doc)
            ).wait_send()

    for step in range(ITERS):
        begun += s_all(step)
        if step + 1 < ITERS:
            begun += [*p_all(step), norm_all(step)]
    for copy in begun:
        copy.wait_send()
    for hop in range(1, num_doc):
        if hop == min(2, num_doc - 1):
            ch_c.all_of(ITERS - 1, ch_c.rows(cbuf, ITERS - 1)).wait_recv()
            m_ref[...] = cbuf[ITERS - 1, :, 0].reshape(n, C)
            for step in range(ITERS):
                ch_y.all_of(step, ch_y.rows(yrecv, step)).wait_send()
                ch_c.all_of(step, ch_c.rows(cbuf, step)).wait_send()
        for s in range(subs):

            @pl.when(me >= hop)
            def _(hop=hop, s=s):
                for copy in w_copy(0, me - hop, s, me):
                    copy.wait_recv()

                @pl.when(me + 1 < num_doc)
                def _():
                    for copy in w_copy(0, me - hop, s, me + 1):
                        copy.start()

                w_write(me - hop, s)

            @pl.when(me + hop < num_doc)
            def _(hop=hop, s=s):
                for copy in w_copy(1, me + hop, s, me):
                    copy.wait_recv()

                @pl.when(me >= 1)
                def _():
                    for copy in w_copy(1, me + hop, s, me - 1):
                        copy.start()

                w_write(me + hop, s)

    for count in range(1, num_doc):

        @pl.when(me + 1 == count)
        def _(count=count):
            w_sent(0, count)

        @pl.when(me + count == num_doc)
        def _(count=count):
            w_sent(1, count)


def whole_kernel(
    num_doc, num_feat, subs, dir_subs, scale,
    docs_ref, dir_ref, phase_hbm, amp_hbm, lab_hbm, dw_hbm,
    m_ref, w_ref,
    feat_ref, featt_ref, gram_ref, inv_ref,
    lab_ref, dw_ref, signs_ref, weight_ref, start_ref, small_sems,
    *scratch,
):
    n = gram_ref.shape[0]
    smalls = [
        pltpu.make_async_copy(lab_hbm, lab_ref, small_sems.at[0]),
        pltpu.make_async_copy(dw_hbm, dw_ref, small_sems.at[1]),
    ]
    for small in smalls:
        small.start()

    def prepare():
        for small in smalls:
            small.wait()
        classes = lax.broadcasted_iota(jnp.int32, (n, C), 1).astype(jnp.float32)
        spread = jnp.broadcast_to(lab_ref[...].astype(jnp.float32), (C, n)).T
        weight = jnp.broadcast_to(dw_ref[...], (C, n)).T
        signs = jnp.where(spread == classes, 1.0, -1.0)
        signs_ref[...] = signs
        weight_ref[...] = weight
        start_ref[...] = logistic_prox(jnp.zeros((n, C), jnp.float32), signs, weight)

    begun = build_kernel(
        num_doc, num_feat, dir_subs, scale, prepare,
        docs_ref, dir_ref, phase_hbm, amp_hbm, feat_ref, featt_ref, gram_ref, *scratch[:13],
    )
    inv_ref[...] = three_left(invert(gram_ref[...]))
    admm_kernel(
        num_doc, num_feat, subs, begun,
        feat_ref, featt_ref, inv_ref, signs_ref, weight_ref, start_ref, m_ref, w_ref,
        *scratch[13:],
    )


def hand_over(margins_ref, weights_ref, m_ref, w_ref, sems):
    copies = [
        pltpu.make_async_copy(margins_ref, m_ref, sems.at[0]),
        pltpu.make_async_copy(weights_ref, w_ref, sems.at[1]),
    ]
    for copy in copies:
        copy.start()
    for copy in copies:
        copy.wait()


def per_device(documents, directions, phase, amplitude, doc_weight, labels):
    n, local_inputs = documents.shape
    input_rows, width_tile = directions.shape
    num_feat = lax.axis_size("feat")
    num_doc = lax.axis_size("doc")
    chunk = width_tile // num_doc
    subs = max(1, min(2, chunk // 128))
    dir_subs = max(1, min(DIR_SUBS, chunk // 128))
    share = n // num_feat
    f32, bf16 = jnp.float32, jnp.bfloat16
    vmem = pl.BlockSpec(memory_space=pltpu.VMEM)
    dma = pltpu.SemaphoreType.DMA
    shape = jax.ShapeDtypeStruct
    rounds = ITERS - 1
    anywhere = pl.BlockSpec(memory_space=pl.ANY)
    groups = max(1, chunk // subs // n)
    operands = (
        documents.T,
        directions,
        phase.reshape(num_doc, 1, chunk),
        amplitude.reshape(num_doc, 1, chunk),
        labels.reshape(1, n),
        doc_weight.reshape(1, n),
    )
    margins, weights = pl.pallas_call(
        functools.partial(
            whole_kernel, num_doc, num_feat, subs, dir_subs, (2.0 / width_tile) ** 0.5
        ),
        out_shape=(shape((n, C), f32), shape((width_tile, C), f32)),
        in_specs=[anywhere] * 6,
        out_specs=(vmem, vmem),
        scratch_shapes=[
            pltpu.VMEM((2, num_doc * n, chunk), bf16),
            pltpu.VMEM((2, chunk, num_doc * n), bf16),
            pltpu.VMEM((n, n), f32),
            pltpu.VMEM((n, 3 * n), bf16),
            pltpu.VMEM((1, n), jnp.int32),
            pltpu.VMEM((1, n), f32),
            pltpu.VMEM((n, C), f32),
            pltpu.VMEM((n, C), f32),
            pltpu.VMEM((n, C), f32),
            dma((2,)),
            pltpu.VMEM((num_feat, num_doc, local_inputs, n), bf16),
            pltpu.VMEM((1, chunk), f32),
            pltpu.VMEM((1, chunk), f32),
            pltpu.VMEM((num_doc, input_rows, chunk), bf16),
            pltpu.VMEM((num_doc, n, n), f32),
            pltpu.VMEM((num_doc, n // 2 + 8, n), f32),
            pltpu.VMEM((num_doc, n // 2 + 8, n), f32),
            dma((2, 1)),
            dma((2, 1)),
            dma((2, dir_subs)),
            dma((2, 1)),
            dma,
            dma((3,)),
            pltpu.VMEM((ITERS, num_doc, n, C), jnp.int16),
            pltpu.VMEM((ITERS, num_doc, 1, C), f32),
            pltpu.VMEM((ITERS, n, C), f32),
            pltpu.VMEM((ITERS, num_feat, share, C), f32),
            pltpu.VMEM((ITERS, num_feat, 2, share, C), f32),
            pltpu.VMEM((rounds, num_doc, n, C), jnp.int16),
            pltpu.VMEM((rounds, num_doc, 1, C), f32),
            pltpu.VMEM((rounds, num_doc, n, C), jnp.int16),
            pltpu.VMEM((rounds, num_doc, 1, C), f32),
            pltpu.VMEM((rounds, num_doc * num_feat, 2, C), f32),
            pltpu.VMEM((chunk, C), f32),
            pltpu.VMEM((chunk, C), f32),
            pltpu.VMEM((chunk, C), f32),
            pltpu.VMEM((num_doc, subs, chunk // subs, C), jnp.int16),
            pltpu.VMEM((num_doc, subs, groups, 1, C), f32),
            dma((2, 2 * ITERS)),
            dma((2, ITERS)),
            dma((2, ITERS)),
            dma((2, 2 * rounds)),
            dma((2, rounds)),
            dma((2, 2)),
            dma((2, num_doc, subs)),
        ],
        compiler_params=pltpu.CompilerParams(
            collective_id=0, has_side_effects=True, vmem_limit_bytes=48 * 1024 * 1024
        ),
        name="admm",
    )(*[pltpu.with_memory_space_constraint(operand, pltpu.HBM) for operand in operands])
    return pl.pallas_call(
        hand_over,
        out_shape=(shape((n, C), f32), shape((width_tile, C), f32)),
        in_specs=[anywhere] * 2,
        out_specs=(anywhere,) * 2,
        scratch_shapes=[dma((2,))],
        compiler_params=pltpu.CompilerParams(vmem_limit_bytes=1024 * 1024),
        name="hand_over",
    )(margins, weights)


def solution(mesh):
    in_specs = (P("doc", "feat"), P("doc", "feat"), P("feat"), P("feat"), P("doc"), P("doc"))
    out_specs = (P("doc", None), P("feat", None))
    return jax.shard_map(
        per_device, mesh=mesh, in_specs=in_specs, out_specs=out_specs, check_vma=False
    )
```
